32 devices in a mesh: row: 8 (over y, x, core), col: 4 (over z).
Axes of the slice: x: 2, y: 2, z: 4, core: 2. Of those that a mesh axis runs over, the one named last changes fastest.
Arguments:
- amplitudes: bfloat16 [2048, 8192], P('row', 'col'), may hold values from -0.125 to 0.125
- integrals: bfloat16 [8192, 1024], P('col', 'row'), may hold values from -6 to 6
- occ_irrep: int32 [200], replicated, may hold values from 0 to 3
- vir_irrep: int32 [6], replicated, may hold values from 0 to 3
- occ_energy: float32 [200], replicated, may hold values from -1 to -0.3
- vir_energy: float32 [1536], replicated, may hold values from 0.2 to 1.5
Outputs:
- update: float32 [2048, 1024], P('row', 'col')
The draws below stay inside these ranges and needn't reach their ends.
All inputs are finite; a program needn't handle non-finite values.
Results may differ from the reference program's by a relative error of at most 0.0003.
Values may be sent and summed in bfloat16 or wider, within the bound.
A program may use at most 128 MiB of HBM per device.

```python
import jax
import jax.numpy as jnp
from jax import lax

NV = 1536
NOCC = 200
TILE = 256
NIRR = 4
NVT = 6
P_ROWS = 2048
K_COLS = 8192
Q_COLS = 1024


def with_ends(values, rng, least, top_value):
    longest = values.shape.index(max(values.shape))
    spots = []
    for shift in (0, 1):
        where = [jax.random.randint(jax.random.fold_in(rng, axis), (), 0, length) for axis, length in enumerate(values.shape)]
        where[longest] = (where[longest] + shift) % values.shape[longest]
        spots.append(tuple(where))
    return values.at[spots[0]].set(least).at[spots[1]].set(top_value)


def steps_of(own_key, extent, shards, smallest, top_value):
    def one(position, shards_of):
        heights = jax.random.uniform(jax.random.fold_in(jax.random.fold_in(own_key, 6), position), (shards_of,), jnp.float32, smallest / len(shards), top_value / len(shards))
        return jnp.repeat(jnp.exp(heights), extent[position] // shards_of).reshape((-1,) + (1,) * (len(extent) - position - 1))

    gain = one(*shards[0])
    for cut in shards[1:]:
        gain = gain * one(*cut)
    return gain


def noise(rng, dims, deviation, most, pieces=(), kind=jnp.bfloat16):
    factor_of = steps_of(rng, dims, pieces, -0.22, 0.18) if pieces else 1.0
    result = jax.random.normal(rng, dims, jnp.float32) * deviation * factor_of
    return jnp.minimum(jnp.maximum(result, -most), most).astype(kind)


def setup_inputs(seed: int = 0) -> dict:
    seeds = jax.random.split(jax.random.key(seed), 7)
    amplitudes = noise(seeds[0], (P_ROWS, K_COLS), (K_COLS // NIRR) ** -0.5, 0.125, ((0, 8), (1, 4)))
    integrals = noise(seeds[1], (K_COLS, Q_COLS), 1.0, 6.0, ((0, 4), (1, 8)))
    occ_irrep = with_ends(jax.random.randint(seeds[2], (NOCC,), 0, NIRR), jax.random.fold_in(seeds[2], 1), 0, NIRR - 1).astype(jnp.int32)
    vir_irrep = with_ends(jax.random.randint(seeds[3], (NVT,), 0, NIRR), jax.random.fold_in(seeds[3], 1), 0, NIRR - 1).astype(jnp.int32)
    occ_energy = jnp.clip(jax.random.uniform(seeds[4], (NOCC,), jnp.float32, -1.0, -0.3), -1.0, -0.3)
    vir_energy = jnp.clip(jax.random.uniform(seeds[5], (NV,), jnp.float32, 0.2, 1.5), 0.2, 1.5)
    return {"amplitudes": amplitudes, "integrals": integrals, "occ_irrep": occ_irrep, "vir_irrep": vir_irrep, "occ_energy": occ_energy, "vir_energy": vir_energy}


def irreps(count, occ_irrep, vir_irrep):
    tiles = jnp.arange(count, dtype=jnp.int32)
    return jnp.bitwise_xor(occ_irrep[tiles // NVT], vir_irrep[tiles % NVT])


def masked(matrix, row_irr, col_irr):
    keep = (row_irr[:, None] == col_irr[None, :]).astype(jnp.float32)
    rows, cols = matrix.shape
    blocks = matrix.astype(jnp.float32).reshape(rows // TILE, TILE, cols // TILE, TILE)
    return (blocks * keep[:, None, :, None]).reshape(rows, cols)


def pair_energy(count, occ_energy, vir_energy):
    index = jnp.arange(count, dtype=jnp.int32)
    return vir_energy[index % NV] - occ_energy[index // NV]


def reference(amplitudes, integrals, occ_irrep, vir_irrep, occ_energy, vir_energy):
    p_irr = irreps(P_ROWS // TILE, occ_irrep, vir_irrep)
    k_irr = irreps(K_COLS // TILE, occ_irrep, vir_irrep)
    q_irr = irreps(Q_COLS // TILE, occ_irrep, vir_irrep)
    masked_amp = masked(amplitudes, p_irr, k_irr)
    masked_int = masked(integrals, k_irr, q_irr)
    cycle = jnp.dot(masked_amp, masked_int, precision=lax.Precision.HIGHEST, preferred_element_type=jnp.float32)
    denom = pair_energy(P_ROWS, occ_energy, vir_energy)[:, None] + pair_energy(Q_COLS, occ_energy, vir_energy)[None, :]
    return cycle / denom
```

```python
import functools

import jax
import jax.numpy as jnp
from jax import lax
from jax.experimental import pallas as pl
from jax.experimental.pallas import tpu as pltpu
from jax.sharding import PartitionSpec as P

TILE = 256
MESH = pl.DeviceIdType.MESH


def lookup(table, index):
    hits = index[:, None] == jnp.arange(table.shape[0], dtype=jnp.int32)[None, :]
    return jnp.sum(jnp.where(hits, table[None, :], jnp.zeros_like(table)[None, :]), axis=1)


def irreps(first_tile, count, occ_irrep, vir_irrep, tiles_virtual):
    tiles = first_tile + jnp.arange(count, dtype=jnp.int32)
    return jnp.bitwise_xor(
        lookup(occ_irrep, tiles // tiles_virtual), lookup(vir_irrep, tiles % tiles_virtual)
    )


def general(amplitudes, integrals, occ_irrep, vir_irrep, occ_energy, vir_energy):
    tile_size = TILE
    tiles_virtual = vir_irrep.shape[0]
    virtual_count = vir_energy.shape[0]
    p_rows, k_cols = amplitudes.shape
    p_tiles = p_rows // tile_size
    k_tiles = k_cols // tile_size
    row_index = lax.axis_index("row")
    col_index = lax.axis_index("col")
    p_irr = irreps(row_index * p_tiles, p_tiles, occ_irrep, vir_irrep, tiles_virtual)
    k_irr = irreps(col_index * k_tiles, k_tiles, occ_irrep, vir_irrep, tiles_virtual)
    match = p_irr[:, None] == k_irr[None, :]
    masked_amp = (
        amplitudes.reshape(p_tiles, tile_size, k_tiles, tile_size)
        * match[:, None, :, None].astype(jnp.bfloat16)
    ).reshape(p_rows, k_cols)
    piece = lax.all_gather(integrals, "row", axis=1, tiled=True)
    width = piece.shape[1]
    columns = jnp.arange(width, dtype=jnp.int32)
    column_tiles = columns // tile_size
    q_irr = jnp.bitwise_xor(
        lookup(occ_irrep, column_tiles // tiles_virtual),
        lookup(vir_irrep, column_tiles % tiles_virtual),
    )
    keeper = (k_irr[:, None] == q_irr[None, :]).astype(jnp.bfloat16)
    masked_int = (piece.reshape(k_tiles, tile_size, width) * keeper[:, None, :]).reshape(
        k_cols, width
    )
    partial_cycle = jnp.dot(masked_amp, masked_int, preferred_element_type=jnp.float32)
    cycle = lax.psum_scatter(partial_cycle, "col", scatter_dimension=1, tiled=True)
    q_cols = cycle.shape[1]
    row_pairs = row_index * p_rows + jnp.arange(p_rows, dtype=jnp.int32)
    col_pairs = col_index * q_cols + jnp.arange(q_cols, dtype=jnp.int32)
    row_energy = lookup(vir_energy, row_pairs % virtual_count) - lookup(
        occ_energy, row_pairs // virtual_count
    )
    col_energy = lookup(vir_energy, col_pairs % virtual_count) - lookup(
        occ_energy, col_pairs // virtual_count
    )
    return cycle / (row_energy[:, None] + col_energy[None, :])


CHUNKS = 4
COLS = 128
SLOTS = (3, 4, 5)
TOP = 32767.0
CODE_ROWS = TILE + 16


def select_tiles(k_irr, irrep, slots):
    tiles = len(k_irr)
    found = [jnp.int32(tiles)] * slots
    count = jnp.int32(0)
    for tile in range(tiles):
        hit = k_irr[tile] == irrep
        found = [
            jnp.where(jnp.logical_and(hit, count == s), tile, found[s]) for s in range(slots)
        ]
        count = count + jnp.where(hit, 1, 0)
    return found


def cycle_kernel(
    nz,
    slots,
    pairs,
    amp_hbm,
    int_hbm,
    occ_irr_hbm,
    vir_irr_hbm,
    occ_e_hbm,
    vir_e_hbm,
    out_ref,
    occ_irr,
    vir_irr,
    occ_e,
    vir_e,
    mine,
    blocks,
    amp,
    own,
    codes,
    in_codes,
    other,
    inverse,
    small_sem,
    int_sem,
    amp_sem,
    near_send,
    near_recv,
    fwd_send,
    z_send,
    z_recv,
    last_sem,
):
    r = lax.axis_index("row")
    z = lax.axis_index("col")
    core = r % 2
    chip = r // 2
    x = chip % 2
    y = chip // 2
    chip_x = chip + 1 - 2 * x
    chip_y = chip + 2 - 4 * y
    chips = (chip, chip_x, chip_y, chip_x + chip_y - chip)
    xr = 2 * chip_x + core
    yr = 2 * chip_y + core
    sr = r + 1 - 2 * core
    tiles_virtual = vir_irr.shape[0]
    k_tiles = mine.shape[0]
    zero_tile = 2 * k_tiles
    step = slots * TILE // CHUNKS

    def remote(src, dst, send_sem, recv_sem, target):
        return pltpu.make_async_remote_copy(
            src_ref=src,
            dst_ref=dst,
            send_sem=send_sem,
            recv_sem=recv_sem,
            device_id=target,
            device_id_type=MESH,
        )

    irr_copies = [
        pltpu.make_async_copy(occ_irr_hbm, occ_irr, small_sem.at[0]),
        pltpu.make_async_copy(vir_irr_hbm, vir_irr, small_sem.at[1]),
    ]
    energy_copies = [
        pltpu.make_async_copy(occ_e_hbm, occ_e, small_sem.at[2]),
        pltpu.make_async_copy(vir_e_hbm, vir_e, small_sem.at[3]),
    ]
    int_copies = []
    amp_copies = []
    amp_shares = []
    for tile in range(k_tiles):
        here = pl.ds(tile * TILE, TILE)
        place = amp.at[core * k_tiles + tile]
        int_copies.append(
            pltpu.make_async_copy(int_hbm.at[here], mine.at[tile], int_sem.at[tile])
        )
        amp_copies.append(
            pltpu.make_async_copy(amp_hbm.at[:, here], place, amp_sem.at[0, tile])
        )
        amp_shares.append(
            remote(
                amp_hbm.at[:, here], place, amp_sem.at[1, tile], amp_sem.at[2, tile], (sr, z)
            )
        )
    for copy in (*irr_copies, *int_copies, *amp_copies, *energy_copies):
        copy.start()

    barrier = pltpu.get_barrier_semaphore()
    for target in (xr, yr, sr):
        pl.semaphore_signal(barrier, inc=1, device_id=(target, z), device_id_type=MESH)
    for k in range(1, nz):
        pl.semaphore_signal(barrier, inc=1, device_id=(r, (z + k) % nz), device_id_type=MESH)

    for copy in irr_copies:
        copy.wait()

    def irrep(number):
        return occ_irr[number // tiles_virtual] ^ vir_irr[number % tiles_virtual]

    k_irr = [irrep(z * k_tiles + tile) for tile in range(k_tiles)]
    q_irr = [irrep(source) for source in chips]
    chosen = [select_tiles(k_irr, q_irr[0], slots)]

    for copy in int_copies:
        copy.wait()
    for s in range(slots):
        tile = jnp.minimum(chosen[0][s], k_tiles - 1)
        blocks[chip, pl.ds(s * TILE, TILE)] = mine[tile]

    pl.semaphore_wait(barrier, 3 + nz - 1)

    half = CHUNKS // 2
    x_order = list(range(CHUNKS))
    y_order = x_order[half:] + x_order[:half]

    def piece(source, chunk):
        return blocks.at[source, pl.ds(chunk * step, step)]

    def near(axis, chunk):
        ref = piece(chip, chunk)
        return remote(
            ref, ref, near_send.at[axis, chunk], near_recv.at[axis, chunk], ((xr, yr)[axis], z)
        )

    def arrival(rel, chunk):
        ref = piece(chips[rel], chunk)
        return remote(ref, ref, near_send.at[0, chunk], near_recv.at[rel - 1, chunk], (xr, z))

    def forward(chunk):
        source, target = (chip_x, yr) if chunk < half else (chip_y, xr)
        ref = piece(source, chunk)
        return remote(ref, ref, fwd_send.at[chunk], near_recv.at[2, chunk], (target, z))

    for cx, cy in zip(x_order, y_order):
        near(0, cx).start()
        near(1, cy).start()

    for copy in amp_shares:
        copy.start()
    amp[zero_tile] = jnp.zeros((TILE, TILE), jnp.bfloat16)
    chosen += [select_tiles(k_irr, q_irr[rel], slots) for rel in (1, 2, 3)]
    first_irr = irrep(2 * chip)
    if pairs == 2:
        sides = [(0, 1)] * 4
    else:
        sides = [(jnp.where(first_irr == q_irr[rel], 0, 1),) for rel in range(4)]
    for copy in amp_copies:
        copy.wait()
    for copy in amp_shares:
        copy.wait_recv()

    def send(rel, side):
        return remote(
            codes.at[rel, side],
            in_codes.at[z, side],
            z_send.at[rel, side],
            z_recv.at[z, side],
            (r, chips[rel]),
        )

    def multiply(rel):
        for side in range(pairs):
            row = sides[rel][side]
            left = jnp.concatenate(
                [
                    amp[jnp.where(tile == k_tiles, zero_tile, row * k_tiles + tile)]
                    for tile in chosen[rel]
                ],
                axis=1,
            )
            product = jnp.dot(left, blocks[chips[rel]], preferred_element_type=jnp.float32)

            @pl.when(z == chips[rel])
            def _():
                own[side] = product

            @pl.when(z != chips[rel])
            def _():
                groups = product.reshape(TILE // 8, 8, COLS)
                most = jnp.maximum(jnp.max(jnp.abs(groups), axis=0), 1e-30)
                power = jnp.ceil(jnp.log2(most))
                scaled = jnp.floor(groups * (TOP * jnp.exp2(-power))[None] + 0.5)
                ints = jnp.clip(scaled, -TOP, TOP).astype(jnp.int32)
                codes[rel, side, pl.ds(0, TILE)] = ints.reshape(TILE, COLS).astype(jnp.int16)
                powers = jnp.concatenate([power, power], axis=0).astype(jnp.int32)
                codes[rel, side, pl.ds(TILE, 16)] = powers.astype(jnp.int16)
                send(rel, side).start()

    multiply(0)
    for cx, cy in zip(x_order, y_order):
        arrival(1, cx).wait_recv()
        if cx < half:
            forward(cx).start()
        arrival(2, cy).wait_recv()
        if cy >= half:
            forward(cy).start()
    multiply(1)
    multiply(2)

    for copy in energy_copies:
        copy.wait()
    v_row = vir_e[:, pl.ds(pl.multiple_of((r % tiles_virtual) * TILE, TILE), TILE)]
    v_col = vir_e[:, pl.ds(pl.multiple_of((z % tiles_virtual) * TILE, TILE), TILE)]
    row_energy = v_row - occ_e[r // tiles_virtual]
    col_energy = v_col - occ_e[z // tiles_virtual]
    keep = jnp.where(irrep(r) == irrep(z), 1.0, 0.0).astype(jnp.float32)
    inverse[...] = keep / (jnp.broadcast_to(row_energy, (TILE, TILE)).T + col_energy)

    for i in range(half):
        for chunk in (i, i + half):
            arrival(3, chunk).wait_recv()
    multiply(3)

    for side in range(pairs):
        total = own[side]
        for k in range(1, nz):
            source = (z + k) % nz
            ref = in_codes.at[source, side]
            remote(
                ref, ref, z_send.at[0, side], z_recv.at[source, side], (r, source)
            ).wait_recv()
            values = in_codes[source, side, pl.ds(0, TILE)].astype(jnp.int32)
            values = values.astype(jnp.float32).reshape(TILE // 8, 8, COLS)
            powers = in_codes[source, side, pl.ds(TILE, 16)].astype(jnp.int32)
            scale = jnp.exp2(powers.astype(jnp.float32)[:8]) * (1.0 / TOP)
            total = total + (values * scale[None]).reshape(TILE, COLS)
        own[side] = total

    kept = core if pairs == 2 else 0
    given = 1 - core if pairs == 2 else 0
    share = remote(own.at[given], other, last_sem.at[0], last_sem.at[1], (sr, z))
    share.start()
    mine_at = pl.ds(pl.multiple_of(core * COLS, COLS), COLS)
    other_at = pl.ds(pl.multiple_of((1 - core) * COLS, COLS), COLS)
    out_ref[:, mine_at] = own[kept] * inverse[:, mine_at]
    share.wait_recv()
    out_ref[:, other_at] = other[...] * inverse[:, other_at]

    for rel in range(4):

        @pl.when(z != chips[rel])
        def _():
            for side in range(pairs):
                send(rel, side).wait_send()

    for chunk in range(CHUNKS):
        near(0, chunk).wait_send()
        near(1, chunk).wait_send()
        forward(chunk).wait_send()
    for copy in amp_shares:
        copy.wait_send()
    share.wait_send()


def fused(nz, slots, pairs, number, amplitudes, integrals, occ_irrep, vir_irrep, occ_energy, vir_energy):
    rows, depth = amplitudes.shape
    k_tiles = depth // TILE
    vmem = pl.BlockSpec(memory_space=pltpu.VMEM)
    hbm = pl.BlockSpec(memory_space=pltpu.HBM)
    dma = pltpu.SemaphoreType.DMA
    return pl.pallas_call(
        functools.partial(cycle_kernel, nz, slots, pairs),
        out_shape=jax.ShapeDtypeStruct((rows, TILE), jnp.float32),
        in_specs=[hbm] * 6,
        out_specs=vmem,
        scratch_shapes=[
            pltpu.SMEM(occ_irrep.shape, jnp.int32),
            pltpu.SMEM(vir_irrep.shape, jnp.int32),
            pltpu.SMEM(occ_energy.shape, jnp.float32),
            pltpu.VMEM((1, vir_energy.shape[0]), jnp.float32),
            pltpu.VMEM((k_tiles, TILE, COLS), jnp.bfloat16),
            pltpu.VMEM((4, slots * TILE, COLS), jnp.bfloat16),
            pltpu.VMEM((2 * k_tiles + 1, rows, TILE), jnp.bfloat16),
            pltpu.VMEM((pairs, rows, COLS), jnp.float32),
            pltpu.VMEM((4, pairs, CODE_ROWS, COLS), jnp.int16),
            pltpu.VMEM((nz, pairs, CODE_ROWS, COLS), jnp.int16),
            pltpu.VMEM((rows, COLS), jnp.float32),
            pltpu.VMEM((rows, TILE), jnp.float32),
            dma((4,)),
            dma((k_tiles,)),
            dma((3, k_tiles)),
            dma((2, CHUNKS)),
            dma((3, CHUNKS)),
            dma((CHUNKS,)),
            dma((4, pairs)),
            dma((nz, pairs)),
            dma((2,)),
        ],
        compiler_params=pltpu.CompilerParams(
            collective_id=number, has_side_effects=True, vmem_limit_bytes=48 << 20
        ),
    )(amplitudes, integrals, occ_irrep, vir_irrep, occ_energy, vir_energy.reshape(1, -1))


def choice_kernel(nz, k_tiles, rows, occ_irr, vir_irr, choice):
    tiles_virtual = vir_irr.shape[0]

    def irrep(number):
        return occ_irr[number // tiles_virtual] ^ vir_irr[number % tiles_virtual]

    q_irr = [irrep(number) for number in range(nz)]
    worst = jnp.int32(0)
    for part in range(nz):
        k_irr = [irrep(part * k_tiles + tile) for tile in range(k_tiles)]
        for q in range(nz):
            count = jnp.int32(0)
            for tile in range(k_tiles):
                count = count + jnp.where(k_irr[tile] == q_irr[q], 1, 0)
            worst = jnp.maximum(worst, count)
    which = jnp.int32(0)
    for slots in SLOTS:
        which = which + jnp.where(worst > slots, 1, 0)
    both = jnp.int32(0)
    for row in range(0, rows, 2):
        first = irrep(row)
        wanted = jnp.int32(0)
        for q in range(nz):
            wanted = wanted + jnp.where(q_irr[q] == first, 1, 0)
        clash = jnp.logical_and(irrep(row + 1) == first, wanted > 0)
        both = jnp.where(clash, 1, both)
    choice[0] = which + both * (len(SLOTS) + 1)


def block_sparse(nz, rows, *args):
    k_tiles = args[0].shape[1] // TILE
    smem = pl.BlockSpec(memory_space=pltpu.SMEM)
    choice = pl.pallas_call(
        functools.partial(choice_kernel, nz, k_tiles, rows),
        out_shape=jax.ShapeDtypeStruct((1,), jnp.int32),
        in_specs=[smem, smem],
        out_specs=smem,
    )(args[2], args[3])[0]
    kinds = [(slots, pairs) for pairs in (1, 2) for slots in (*SLOTS, k_tiles)]
    branches = [
        functools.partial(fused, nz, slots, pairs, number)
        for number, (slots, pairs) in enumerate(kinds)
    ]
    return lax.switch(choice, branches, *args)


def solution(mesh):
    row, col = mesh.shape["row"], mesh.shape["col"]

    def shards(amplitudes, integrals, occ_irrep, vir_irrep, occ_energy, vir_energy):
        args = (amplitudes, integrals, occ_irrep, vir_irrep, occ_energy, vir_energy)
        plain = (
            (row, col) == (8, 4)
            and amplitudes.shape[0] == TILE
            and integrals.shape[1] == COLS
            and vir_energy.shape[0] == TILE * vir_irrep.shape[0]
        )
        return block_sparse(col, row, *args) if plain else general(*args)

    return jax.shard_map(
        shards,
        mesh=mesh,
        in_specs=(P("row", "col"), P("col", "row"), P(), P(), P(), P()),
        out_specs=P("row", "col"),
        check_vma=False,
    )
```

```python
import functools

import jax
import jax.numpy as jnp
from jax import lax
from jax.experimental import pallas as pl
from jax.experimental.pallas import tpu as pltpu
from jax.sharding import PartitionSpec as P

TILE = 256
MESH = pl.DeviceIdType.MESH


def lookup(table, index):
    hits = index[:, None] == jnp.arange(table.shape[0], dtype=jnp.int32)[None, :]
    return jnp.sum(jnp.where(hits, table[None, :], jnp.zeros_like(table)[None, :]), axis=1)


def irreps(first_tile, count, occ_irrep, vir_irrep, tiles_virtual):
    tiles = first_tile + jnp.arange(count, dtype=jnp.int32)
    return jnp.bitwise_xor(
        lookup(occ_irrep, tiles // tiles_virtual), lookup(vir_irrep, tiles % tiles_virtual)
    )


def general(amplitudes, integrals, occ_irrep, vir_irrep, occ_energy, vir_energy):
    tile_size = TILE
    tiles_virtual = vir_irrep.shape[0]
    virtual_count = vir_energy.shape[0]
    p_rows, k_cols = amplitudes.shape
    p_tiles = p_rows // tile_size
    k_tiles = k_cols // tile_size
    row_index = lax.axis_index("row")
    col_index = lax.axis_index("col")
    p_irr = irreps(row_index * p_tiles, p_tiles, occ_irrep, vir_irrep, tiles_virtual)
    k_irr = irreps(col_index * k_tiles, k_tiles, occ_irrep, vir_irrep, tiles_virtual)
    match = p_irr[:, None] == k_irr[None, :]
    masked_amp = (
        amplitudes.reshape(p_tiles, tile_size, k_tiles, tile_size)
        * match[:, None, :, None].astype(jnp.bfloat16)
    ).reshape(p_rows, k_cols)
    piece = lax.all_gather(integrals, "row", axis=1, tiled=True)
    width = piece.shape[1]
    columns = jnp.arange(width, dtype=jnp.int32)
    column_tiles = columns // tile_size
    q_irr = jnp.bitwise_xor(
        lookup(occ_irrep, column_tiles // tiles_virtual),
        lookup(vir_irrep, column_tiles % tiles_virtual),
    )
    keeper = (k_irr[:, None] == q_irr[None, :]).astype(jnp.bfloat16)
    masked_int = (piece.reshape(k_tiles, tile_size, width) * keeper[:, None, :]).reshape(
        k_cols, width
    )
    partial_cycle = jnp.dot(masked_amp, masked_int, preferred_element_type=jnp.float32)
    cycle = lax.psum_scatter(partial_cycle, "col", scatter_dimension=1, tiled=True)
    q_cols = cycle.shape[1]
    row_pairs = row_index * p_rows + jnp.arange(p_rows, dtype=jnp.int32)
    col_pairs = col_index * q_cols + jnp.arange(q_cols, dtype=jnp.int32)
    row_energy = lookup(vir_energy, row_pairs % virtual_count) - lookup(
        occ_energy, row_pairs // virtual_count
    )
    col_energy = lookup(vir_energy, col_pairs % virtual_count) - lookup(
        occ_energy, col_pairs // virtual_count
    )
    return cycle / (row_energy[:, None] + col_energy[None, :])


CHUNKS = 4
COLS = 128
SLOTS = (3, 4, 5)
TOP = 32767.0
CODE_ROWS = TILE + 16


def select_tiles(k_irr, irrep, slots):
    tiles = len(k_irr)
    found = [jnp.int32(tiles)] * slots
    count = jnp.int32(0)
    for tile in range(tiles):
        hit = k_irr[tile] == irrep
        found = [
            jnp.where(jnp.logical_and(hit, count == s), tile, found[s]) for s in range(slots)
        ]
        count = count + jnp.where(hit, 1, 0)
    return found


def cycle_kernel(
    nz,
    slots,
    pairs,
    amp_hbm,
    packed,
    occ_irr_in,
    vir_irr_in,
    energies,
    out_ref,
    occ_irr,
    vir_irr,
    blocks,
    amp,
    own,
    codes,
    in_codes,
    other,
    inverse,
    small_sem,
    amp_sem,
    near_send,
    near_recv,
    fwd_send,
    z_send,
    z_recv,
    last_sem,
):
    r = lax.axis_index("row")
    z = lax.axis_index("col")
    core = r % 2
    chip = r // 2
    x = chip % 2
    y = chip // 2
    chip_x = chip + 1 - 2 * x
    chip_y = chip + 2 - 4 * y
    chips = (chip, chip_x, chip_y, chip_x + chip_y - chip)
    xr = 2 * chip_x + core
    yr = 2 * chip_y + core
    sr = r + 1 - 2 * core
    tiles_virtual = vir_irr.shape[0]
    k_tiles = amp_hbm.shape[1] // TILE
    zero_tile = 2 * k_tiles
    step = slots * TILE // CHUNKS

    def remote(src, dst, send_sem, recv_sem, target):
        return pltpu.make_async_remote_copy(
            src_ref=src,
            dst_ref=dst,
            send_sem=send_sem,
            recv_sem=recv_sem,
            device_id=target,
            device_id_type=MESH,
        )

    irr_copies = [
        pltpu.make_async_copy(occ_irr_in, occ_irr, small_sem.at[0]),
        pltpu.make_async_copy(vir_irr_in, vir_irr, small_sem.at[1]),
    ]
    amp_copies = []
    amp_shares = []
    for tile in range(k_tiles):
        here = pl.ds(tile * TILE, TILE)
        place = amp.at[core * k_tiles + tile]
        amp_copies.append(
            pltpu.make_async_copy(amp_hbm.at[:, here], place, amp_sem.at[0, tile])
        )
        amp_shares.append(
            remote(
                amp_hbm.at[:, here], place, amp_sem.at[1, tile], amp_sem.at[2, tile], (sr, z)
            )
        )
    for copy in (*irr_copies, *amp_copies):
        copy.start()

    barrier = pltpu.get_barrier_semaphore()
    for target in (xr, yr, sr):
        pl.semaphore_signal(barrier, inc=1, device_id=(target, z), device_id_type=MESH)
    for k in range(1, nz):
        pl.semaphore_signal(barrier, inc=1, device_id=(r, (z + k) % nz), device_id_type=MESH)

    pl.semaphore_wait(barrier, 3 + nz - 1)

    half = CHUNKS // 2
    x_order = list(range(CHUNKS))
    y_order = x_order[half:] + x_order[:half]

    def piece(source, chunk):
        return blocks.at[source, pl.ds(chunk * step, step)]

    def near(axis, chunk):
        return remote(
            packed.at[pl.ds(chunk * step, step)], piece(chip, chunk), near_send.at[axis, chunk], near_recv.at[axis, chunk], ((xr, yr)[axis], z)
        )

    def arrival(rel, chunk):
        ref = piece(chips[rel], chunk)
        return remote(ref, ref, near_send.at[0, chunk], near_recv.at[rel - 1, chunk], (xr, z))

    def forward(chunk):
        source, target = (chip_x, yr) if chunk < half else (chip_y, xr)
        ref = piece(source, chunk)
        return remote(ref, ref, fwd_send.at[chunk], near_recv.at[2, chunk], (target, z))

    for cx, cy in zip(x_order, y_order):
        near(0, cx).start()
        near(1, cy).start()

    for copy in amp_shares:
        copy.start()
    amp[zero_tile] = jnp.zeros((TILE, TILE), jnp.bfloat16)

    for copy in irr_copies:
        copy.wait()

    def irrep(number):
        return occ_irr[number // tiles_virtual] ^ vir_irr[number % tiles_virtual]

    k_irr = [irrep(z * k_tiles + tile) for tile in range(k_tiles)]
    q_irr = [irrep(source) for source in chips]
    chosen = [select_tiles(k_irr, q_irr[rel], slots) for rel in range(4)]
    first_irr = irrep(2 * chip)
    if pairs == 2:
        sides = [(0, 1)] * 4
    else:
        sides = [(jnp.where(first_irr == q_irr[rel], 0, 1),) for rel in range(4)]
    for copy in amp_copies:
        copy.wait()
    for copy in amp_shares:
        copy.wait_recv()

    def send(rel, side):
        return remote(
            codes.at[rel, side],
            in_codes.at[z, side],
            z_send.at[rel, side],
            z_recv.at[z, side],
            (r, chips[rel]),
        )

    def multiply(rel):
        for side in range(pairs):
            row = sides[rel][side]
            left = jnp.concatenate(
                [
                    amp[jnp.where(tile == k_tiles, zero_tile, row * k_tiles + tile)]
                    for tile in chosen[rel]
                ],
                axis=1,
            )
            right = blocks[chips[rel]] if rel else packed[: slots * TILE]
            product = jnp.dot(left, right, preferred_element_type=jnp.float32)

            @pl.when(z == chips[rel])
            def _():
                own[side] = product

            @pl.when(z != chips[rel])
            def _():
                groups = product.reshape(TILE // 8, 8, COLS)
                most = jnp.maximum(jnp.max(jnp.abs(groups), axis=0), 1e-30)
                power = jnp.ceil(jnp.log2(most))
                scaled = jnp.floor(groups * (TOP * jnp.exp2(-power))[None] + 0.5)
                ints = jnp.clip(scaled, -TOP, TOP).astype(jnp.int32)
                codes[rel, side, pl.ds(0, TILE)] = ints.reshape(TILE, COLS).astype(jnp.int16)
                powers = jnp.concatenate([power, power], axis=0).astype(jnp.int32)
                codes[rel, side, pl.ds(TILE, 16)] = powers.astype(jnp.int16)
                send(rel, side).start()

    multiply(0)
    for cx, cy in zip(x_order, y_order):
        arrival(1, cx).wait_recv()
        if cx < half:
            forward(cx).start()
        arrival(2, cy).wait_recv()
        if cy >= half:
            forward(cy).start()
    multiply(1)
    multiply(2)

    row_energy = jnp.concatenate([energies[0:1], energies[1:2]], axis=1)
    col_energy = jnp.concatenate([energies[2:3], energies[3:4]], axis=1)
    keep = jnp.where(irrep(r) == irrep(z), 1.0, 0.0).astype(jnp.float32)
    inverse[...] = keep / (jnp.broadcast_to(row_energy, (TILE, TILE)).T + col_energy)

    for i in range(half):
        for chunk in (i, i + half):
            arrival(3, chunk).wait_recv()
    multiply(3)

    for side in range(pairs):
        total = own[side]
        for k in range(1, nz):
            source = (z + k) % nz
            ref = in_codes.at[source, side]
            remote(
                ref, ref, z_send.at[0, side], z_recv.at[source, side], (r, source)
            ).wait_recv()
            values = in_codes[source, side, pl.ds(0, TILE)].astype(jnp.int32)
            values = values.astype(jnp.float32).reshape(TILE // 8, 8, COLS)
            powers = in_codes[source, side, pl.ds(TILE, 16)].astype(jnp.int32)
            scale = jnp.exp2(powers.astype(jnp.float32)[:8]) * (1.0 / TOP)
            total = total + (values * scale[None]).reshape(TILE, COLS)
        own[side] = total

    kept = core if pairs == 2 else 0
    given = 1 - core if pairs == 2 else 0
    share = remote(own.at[given], other, last_sem.at[0], last_sem.at[1], (sr, z))
    share.start()
    mine_at = pl.ds(pl.multiple_of(core * COLS, COLS), COLS)
    other_at = pl.ds(pl.multiple_of((1 - core) * COLS, COLS), COLS)
    out_ref[:, mine_at] = own[kept] * inverse[:, mine_at]
    share.wait_recv()
    out_ref[:, other_at] = other[...] * inverse[:, other_at]

    for rel in range(4):

        @pl.when(z != chips[rel])
        def _():
            for side in range(pairs):
                send(rel, side).wait_send()

    for chunk in range(CHUNKS):
        near(0, chunk).wait_send()
        near(1, chunk).wait_send()
        forward(chunk).wait_send()
    for copy in amp_shares:
        copy.wait_send()
    share.wait_send()


def fused(nz, slots, pairs, number, amplitudes, packed, occ_irrep, vir_irrep, energies):
    rows, depth = amplitudes.shape
    k_tiles = depth // TILE
    vmem = pl.BlockSpec(memory_space=pltpu.VMEM)
    hbm = pl.BlockSpec(memory_space=pltpu.HBM)
    dma = pltpu.SemaphoreType.DMA
    return pl.pallas_call(
        functools.partial(cycle_kernel, nz, slots, pairs),
        out_shape=jax.ShapeDtypeStruct((rows, TILE), jnp.float32),
        in_specs=[hbm, vmem, vmem, vmem, vmem],
        out_specs=vmem,
        scratch_shapes=[
            pltpu.SMEM(occ_irrep.shape, jnp.int32),
            pltpu.SMEM(vir_irrep.shape, jnp.int32),
            pltpu.VMEM((4, slots * TILE, COLS), jnp.bfloat16),
            pltpu.VMEM((2 * k_tiles + 1, rows, TILE), jnp.bfloat16),
            pltpu.VMEM((pairs, rows, COLS), jnp.float32),
            pltpu.VMEM((4, pairs, CODE_ROWS, COLS), jnp.int16),
            pltpu.VMEM((nz, pairs, CODE_ROWS, COLS), jnp.int16),
            pltpu.VMEM((rows, COLS), jnp.float32),
            pltpu.VMEM((rows, TILE), jnp.float32),
            dma((2,)),
            dma((3, k_tiles)),
            dma((2, CHUNKS)),
            dma((3, CHUNKS)),
            dma((CHUNKS,)),
            dma((4, pairs)),
            dma((nz, pairs)),
            dma((2,)),
        ],
        compiler_params=pltpu.CompilerParams(
            collective_id=number, has_side_effects=True, vmem_limit_bytes=40 << 20
        ),
    )(amplitudes, packed, occ_irrep, vir_irrep, energies)


def choice_kernel(
    nz,
    k_tiles,
    rows,
    int_hbm,
    occ_irr_hbm,
    vir_irr_hbm,
    occ_e_hbm,
    vir_e_hbm,
    choice,
    packed,
    occ_irr_out,
    vir_irr_out,
    energies,
    mine,
    occ_irr,
    vir_irr,
    occ_e,
    int_sem,
    small_sem,
):
    r = lax.axis_index("row")
    z = lax.axis_index("col")
    tiles_virtual = vir_irr.shape[0]
    half = TILE // 2
    irr_copies = [
        pltpu.make_async_copy(occ_irr_hbm, occ_irr, small_sem.at[0]),
        pltpu.make_async_copy(vir_irr_hbm, vir_irr, small_sem.at[1]),
    ]
    other_copies = [
        pltpu.make_async_copy(occ_irr_hbm, occ_irr_out, small_sem.at[2]),
        pltpu.make_async_copy(vir_irr_hbm, vir_irr_out, small_sem.at[3]),
        pltpu.make_async_copy(occ_e_hbm, occ_e, small_sem.at[4]),
    ]
    for i in range(4):
        tile = (r if i < 2 else z) % tiles_virtual
        start = pl.multiple_of(tile * TILE + (i % 2) * half, half)
        other_copies.append(
            pltpu.make_async_copy(
                vir_e_hbm.at[pl.ds(start, half)], energies.at[i], small_sem.at[5 + i]
            )
        )
    int_copies = []
    for tile in range(k_tiles):
        here = pl.ds(tile * TILE, TILE)
        int_copies.append(
            pltpu.make_async_copy(int_hbm.at[here], mine.at[tile], int_sem.at[tile])
        )
    for copy in (*irr_copies, *int_copies, *other_copies):
        copy.start()
    for copy in irr_copies:
        copy.wait()

    def irrep(number):
        return occ_irr[number // tiles_virtual] ^ vir_irr[number % tiles_virtual]

    chosen = select_tiles(
        [irrep(z * k_tiles + tile) for tile in range(k_tiles)], irrep(r // 2), k_tiles
    )
    q_irr = [irrep(number) for number in range(nz)]
    worst = jnp.int32(0)
    for part in range(nz):
        k_irr = [irrep(part * k_tiles + tile) for tile in range(k_tiles)]
        for q in range(nz):
            count = jnp.int32(0)
            for tile in range(k_tiles):
                count = count + jnp.where(k_irr[tile] == q_irr[q], 1, 0)
            worst = jnp.maximum(worst, count)
    which = jnp.int32(0)
    for slots in SLOTS:
        which = which + jnp.where(worst > slots, 1, 0)
    both = jnp.int32(0)
    for row in range(0, rows, 2):
        first = irrep(row)
        wanted = jnp.int32(0)
        for q in range(nz):
            wanted = wanted + jnp.where(q_irr[q] == first, 1, 0)
        clash = jnp.logical_and(irrep(row + 1) == first, wanted > 0)
        both = jnp.where(clash, 1, both)
    choice[0] = which + both * (len(SLOTS) + 1)

    for copy in int_copies:
        copy.wait()
    for s in range(k_tiles):
        packed[pl.ds(s * TILE, TILE)] = mine[jnp.minimum(chosen[s], k_tiles - 1)]
    for copy in other_copies:
        copy.wait()
    row_occ = occ_e[r // tiles_virtual]
    col_occ = occ_e[z // tiles_virtual]
    energies[0:2] = energies[0:2] - row_occ
    energies[2:4] = energies[2:4] - col_occ


def block_sparse(nz, rows, amplitudes, integrals, occ_irrep, vir_irrep, occ_energy, vir_energy):
    k_tiles = amplitudes.shape[1] // TILE
    smem = pl.BlockSpec(memory_space=pltpu.SMEM)
    vmem = pl.BlockSpec(memory_space=pltpu.VMEM)
    hbm = pl.BlockSpec(memory_space=pltpu.HBM)
    dma = pltpu.SemaphoreType.DMA
    choice, *rest = pl.pallas_call(
        functools.partial(choice_kernel, nz, k_tiles, rows),
        out_shape=[
            jax.ShapeDtypeStruct((1,), jnp.int32),
            jax.ShapeDtypeStruct(integrals.shape, integrals.dtype),
            jax.ShapeDtypeStruct(occ_irrep.shape, jnp.int32),
            jax.ShapeDtypeStruct(vir_irrep.shape, jnp.int32),
            jax.ShapeDtypeStruct((4, TILE // 2), jnp.float32),
        ],
        in_specs=[hbm] * 5,
        out_specs=[smem, vmem, vmem, vmem, vmem],
        scratch_shapes=[
            pltpu.VMEM((k_tiles, TILE, COLS), jnp.bfloat16),
            pltpu.SMEM(occ_irrep.shape, jnp.int32),
            pltpu.SMEM(vir_irrep.shape, jnp.int32),
            pltpu.SMEM(occ_energy.shape, jnp.float32),
            dma((k_tiles,)),
            dma((9,)),
        ],
    )(integrals, occ_irrep, vir_irrep, occ_energy, vir_energy)
    kinds = [(slots, pairs) for pairs in (1, 2) for slots in (*SLOTS, k_tiles)]
    branches = [
        functools.partial(fused, nz, slots, pairs, number)
        for number, (slots, pairs) in enumerate(kinds)
    ]
    return lax.switch(choice[0], branches, amplitudes, *rest)


def solution(mesh):
    row, col = mesh.shape["row"], mesh.shape["col"]

    def shards(amplitudes, integrals, occ_irrep, vir_irrep, occ_energy, vir_energy):
        args = (amplitudes, integrals, occ_irrep, vir_irrep, occ_energy, vir_energy)
        plain = (
            (row, col) == (8, 4)
            and amplitudes.shape[0] == TILE
            and integrals.shape[1] == COLS
            and vir_energy.shape[0] == TILE * vir_irrep.shape[0]
        )
        return block_sparse(col, row, *args) if plain else general(*args)

    return jax.shard_map(
        shards,
        mesh=mesh,
        in_specs=(P("row", "col"), P("col", "row"), P(), P(), P(), P()),
        out_specs=P("row", "col"),
        check_vma=False,
    )
```

```python
import functools

import jax
import jax.numpy as jnp
from jax import lax
from jax.experimental import pallas as pl
from jax.experimental.pallas import tpu as pltpu
from jax.sharding import PartitionSpec as P

TILE = 256
MESH = pl.DeviceIdType.MESH


def lookup(table, index):
    hits = index[:, None] == jnp.arange(table.shape[0], dtype=jnp.int32)[None, :]
    return jnp.sum(jnp.where(hits, table[None, :], jnp.zeros_like(table)[None, :]), axis=1)


def irreps(first_tile, count, occ_irrep, vir_irrep, tiles_virtual):
    tiles = first_tile + jnp.arange(count, dtype=jnp.int32)
    return jnp.bitwise_xor(
        lookup(occ_irrep, tiles // tiles_virtual), lookup(vir_irrep, tiles % tiles_virtual)
    )


def general(amplitudes, integrals, occ_irrep, vir_irrep, occ_energy, vir_energy):
    tile_size = TILE
    tiles_virtual = vir_irrep.shape[0]
    virtual_count = vir_energy.shape[0]
    p_rows, k_cols = amplitudes.shape
    p_tiles = p_rows // tile_size
    k_tiles = k_cols // tile_size
    row_index = lax.axis_index("row")
    col_index = lax.axis_index("col")
    p_irr = irreps(row_index * p_tiles, p_tiles, occ_irrep, vir_irrep, tiles_virtual)
    k_irr = irreps(col_index * k_tiles, k_tiles, occ_irrep, vir_irrep, tiles_virtual)
    match = p_irr[:, None] == k_irr[None, :]
    masked_amp = (
        amplitudes.reshape(p_tiles, tile_size, k_tiles, tile_size)
        * match[:, None, :, None].astype(jnp.bfloat16)
    ).reshape(p_rows, k_cols)
    piece = lax.all_gather(integrals, "row", axis=1, tiled=True)
    width = piece.shape[1]
    columns = jnp.arange(width, dtype=jnp.int32)
    column_tiles = columns // tile_size
    q_irr = jnp.bitwise_xor(
        lookup(occ_irrep, column_tiles // tiles_virtual),
        lookup(vir_irrep, column_tiles % tiles_virtual),
    )
    keeper = (k_irr[:, None] == q_irr[None, :]).astype(jnp.bfloat16)
    masked_int = (piece.reshape(k_tiles, tile_size, width) * keeper[:, None, :]).reshape(
        k_cols, width
    )
    partial_cycle = jnp.dot(masked_amp, masked_int, preferred_element_type=jnp.float32)
    cycle = lax.psum_scatter(partial_cycle, "col", scatter_dimension=1, tiled=True)
    q_cols = cycle.shape[1]
    row_pairs = row_index * p_rows + jnp.arange(p_rows, dtype=jnp.int32)
    col_pairs = col_index * q_cols + jnp.arange(q_cols, dtype=jnp.int32)
    row_energy = lookup(vir_energy, row_pairs % virtual_count) - lookup(
        occ_energy, row_pairs // virtual_count
    )
    col_energy = lookup(vir_energy, col_pairs % virtual_count) - lookup(
        occ_energy, col_pairs // virtual_count
    )
    return cycle / (row_energy[:, None] + col_energy[None, :])


CHUNKS = 4
COLS = 128
SLOTS = (3, 4, 5)
TOP = 32767.0
HALF = TILE // 2
CODE_ROWS = HALF + 16


def select_tiles(k_irr, irrep, slots):
    tiles = len(k_irr)
    found = [jnp.int32(tiles)] * slots
    count = jnp.int32(0)
    for tile in range(tiles):
        hit = k_irr[tile] == irrep
        found = [
            jnp.where(jnp.logical_and(hit, count == s), tile, found[s]) for s in range(slots)
        ]
        count = count + jnp.where(hit, 1, 0)
    return found


def cycle_kernel(
    nz,
    slots,
    pairs,
    amp_hbm,
    packed,
    occ_irr_in,
    vir_irr_in,
    energies,
    out_ref,
    occ_irr,
    vir_irr,
    table,
    blocks,
    amp,
    own,
    codes,
    in_codes,
    other,
    inverse,
    small_sem,
    amp_sem,
    near_send,
    near_recv,
    fwd_send,
    z_send,
    z_recv,
    last_sem,
):
    r = lax.axis_index("row")
    z = lax.axis_index("col")
    core = r % 2
    chip = r // 2
    x = chip % 2
    y = chip // 2
    chip_x = chip + 1 - 2 * x
    chip_y = chip + 2 - 4 * y
    chips = (chip, chip_x, chip_y, chip_x + chip_y - chip)
    xr = 2 * chip_x + core
    yr = 2 * chip_y + core
    sr = r + 1 - 2 * core
    tiles_virtual = vir_irr.shape[0]
    k_tiles = amp_hbm.shape[1] // TILE
    zero_tile = 2 * k_tiles
    depth = slots * HALF
    step = depth // 2

    def remote(src, dst, send_sem, recv_sem, target):
        return pltpu.make_async_remote_copy(
            src_ref=src,
            dst_ref=dst,
            send_sem=send_sem,
            recv_sem=recv_sem,
            device_id=target,
            device_id_type=MESH,
        )

    irr_copies = [
        pltpu.make_async_copy(occ_irr_in, occ_irr, small_sem.at[0]),
        pltpu.make_async_copy(vir_irr_in, vir_irr, small_sem.at[1]),
    ]
    amp_copies = []
    amp_shares = []
    for tile in range(k_tiles):
        here = pl.ds(tile * TILE, TILE)
        place = amp.at[core * k_tiles + tile]
        amp_copies.append(
            pltpu.make_async_copy(amp_hbm.at[:, here], place, amp_sem.at[0, tile])
        )
        amp_shares.append(
            remote(
                amp_hbm.at[:, here], place, amp_sem.at[1, tile], amp_sem.at[2, tile], (sr, z)
            )
        )
    own_copy = pltpu.make_async_copy(
        packed.at[:, pl.ds(0, depth)], blocks.at[chip], small_sem.at[2]
    )
    for copy in (*irr_copies, *amp_copies, own_copy):
        copy.start()

    barrier = pltpu.get_barrier_semaphore()
    for target in (xr, yr, sr):
        pl.semaphore_signal(barrier, inc=1, device_id=(target, z), device_id_type=MESH)
    rows_met = (r,) if pairs == 1 else (r, sr)
    for k in range(1, nz):
        for row in rows_met:
            pl.semaphore_signal(
                barrier, inc=1, device_id=(row, (z + k) % nz), device_id_type=MESH
            )

    pl.semaphore_wait(barrier, 3 + len(rows_met) * (nz - 1))

    x_order = (0, 1, 2, 3)
    y_order = (1, 0, 3, 2)

    def piece(source, chunk):
        return blocks.at[source, chunk // 2, pl.ds(chunk % 2 * step, step)]

    def near(axis, chunk):
        return remote(
            packed.at[chunk // 2, pl.ds(chunk % 2 * step, step)],
            piece(chip, chunk),
            near_send.at[axis, chunk],
            near_recv.at[axis, chunk],
            ((xr, yr)[axis], z),
        )

    def arrival(rel, chunk):
        ref = piece(chips[rel], chunk)
        return remote(ref, ref, near_send.at[0, chunk], near_recv.at[rel - 1, chunk], (xr, z))

    def forward(chunk):
        source, target = (chip_x, yr) if chunk % 2 == 0 else (chip_y, xr)
        ref = piece(source, chunk)
        return remote(ref, ref, fwd_send.at[chunk], near_recv.at[2, chunk], (target, z))

    for cx, cy in zip(x_order[:3], y_order[:3]):
        near(0, cx).start()
        near(1, cy).start()

    for copy in amp_shares:
        copy.start()
    amp[zero_tile] = jnp.zeros((TILE, TILE), jnp.bfloat16)

    for copy in irr_copies:
        copy.wait()

    def irrep(number):
        return occ_irr[number // tiles_virtual] ^ vir_irr[number % tiles_virtual]

    k_irr = [irrep(z * k_tiles + tile) for tile in range(k_tiles)]
    q_irr = [irrep(source) for source in chips]
    first_irr = irrep(2 * chip)
    for rel in range(4):
        chosen = select_tiles(k_irr, q_irr[rel], slots)
        for side in range(pairs):
            row = side if pairs == 2 else jnp.where(first_irr == q_irr[rel], 0, 1)
            for i, tile in enumerate(chosen):
                table[(rel * pairs + side) * slots + i] = jnp.where(
                    tile == k_tiles, zero_tile, row * k_tiles + tile
                )
    own_copy.wait()
    for copy in amp_copies:
        copy.wait()
    for copy in amp_shares:
        copy.wait_recv()

    low = lax.broadcasted_iota(jnp.int32, (HALF, COLS), 1) < COLS // 2

    def swap(values):
        return pltpu.roll(values, COLS // 2, 1)

    def chip_of(rel):
        return (x + rel % 2) % 2 + 2 * ((y + rel // 2) % 2)

    def send(rel, side, part):
        place = 0 if pairs == 1 else core
        row = r if pairs == 1 else 2 * chip + side
        return remote(
            codes.at[rel, side, part],
            in_codes.at[z, place, part],
            z_send.at[rel, side, part],
            z_recv.at[z, place, part],
            (row, chip_of(rel)),
        )

    def share(part):
        given = 0 if pairs == 1 else 1 - core
        return remote(
            own.at[given, part], other.at[part], last_sem.at[0, part], last_sem.at[1, part], (sr, z)
        )

    def multiply(rel, side, part):
        source = chip_of(rel)
        left = jnp.concatenate(
            [amp[table[(rel * pairs + side) * slots + i]] for i in range(slots)], axis=1
        )
        right = blocks[source, part]
        one = jnp.dot(left[:, :depth], right, preferred_element_type=jnp.float32)
        two = jnp.dot(left[:, depth:], right, preferred_element_type=jnp.float32)
        product = jnp.where(
            low, one[:HALF] + swap(two[:HALF]), swap(one[HALF:]) + two[HALF:]
        )

        @pl.when(z == source)
        def _():
            own[side, part] = product

        @pl.when(z != source)
        def _():
            groups = product.reshape(HALF // 16, 16, COLS)
            most = jnp.maximum(jnp.max(jnp.abs(groups), axis=0), 1e-30)
            power = jnp.ceil(jnp.log2(most))
            scaled = jnp.floor(groups * (TOP * jnp.exp2(-power))[None] + 0.5)
            ints = jnp.clip(scaled, -TOP, TOP).astype(jnp.int32)
            codes[rel, side, part, pl.ds(0, HALF)] = ints.reshape(HALF, COLS).astype(jnp.int16)
            codes[rel, side, part, pl.ds(HALF, 16)] = power.astype(jnp.int32).astype(jnp.int16)
            send(rel, side, part).start()

    def pass_on(*chunks):
        for chunk in chunks:
            arrival(1 + chunk % 2, chunk).wait_recv()
            forward(chunk).start()

    def when(turn, number):
        return pl.when(turn == number)

    def turn_body(turn, _):
        rel = jnp.where(turn < 2, 0, (turn + 1) % 3 + 1)
        part = jnp.where(turn < 2, turn, (turn + 1) // 3 - 1)

        @when(turn, 2)
        def _():
            pass_on(0, 1)
            near(0, x_order[3]).start()
            near(1, y_order[3]).start()
            arrival(1, 1).wait_recv()

        @when(turn, 3)
        def _():
            arrival(2, 0).wait_recv()

        @when(turn, 4)
        def _():
            pass_on(2, 3)
            arrival(3, 0).wait_recv()
            arrival(3, 1).wait_recv()

        @when(turn, 5)
        def _():
            row_energy = jnp.concatenate([energies[0:1], energies[1:2]], axis=1)
            col_energy = jnp.concatenate([energies[2:3], energies[3:4]], axis=1)
            keep = jnp.where(irrep(r) == irrep(z), 1.0, 0.0).astype(jnp.float32)
            inverse[...] = keep / (jnp.broadcast_to(row_energy, (TILE, TILE)).T + col_energy)
            arrival(1, 3).wait_recv()

        @when(turn, 6)
        def _():
            arrival(2, 2).wait_recv()

        @when(turn, 7)
        def _():
            arrival(3, 2).wait_recv()
            arrival(3, 3).wait_recv()

        for side in range(pairs):
            multiply(rel, side, part)
        if pairs == 2:

            @pl.when(z == chip_of(rel))
            def _():
                share(part).start()

        return 0

    lax.fori_loop(0, 8, turn_body, 0)

    def collect(total, place, part):
        for k in range(1, nz):
            source = (z + k) % nz
            ref = in_codes.at[source, place, part]
            remote(
                ref, ref, z_send.at[0, 0, part], z_recv.at[source, place, part], (r, source)
            ).wait_recv()
            values = in_codes[source, place, part, pl.ds(0, HALF)].astype(jnp.int32)
            values = values.astype(jnp.float32).reshape(HALF // 16, 16, COLS)
            powers = in_codes[source, place, part, pl.ds(HALF, 16)].astype(jnp.int32)
            scale = jnp.exp2(powers.astype(jnp.float32)) * (1.0 / TOP)
            total = total + (values * scale[None]).reshape(HALF, COLS)
        return total

    def put(half_core, first, last):
        here = pl.ds(pl.multiple_of(half_core * COLS, COLS), COLS)
        top = jnp.where(low, first, swap(last))
        bottom = jnp.where(low, swap(first), last)
        out_ref[:HALF, here] = top * inverse[:HALF, here]
        out_ref[HALF:, here] = bottom * inverse[HALF:, here]

    if pairs == 1:
        for part in (0, 1):
            own[0, part] = collect(own[0, part], 0, part)
            share(part).start()
        put(core, own[0, 0], own[0, 1])
        for part in (0, 1):
            share(part).wait_recv()
        put(1 - core, other[0], other[1])
    else:
        for part in (0, 1):
            share(part).wait_recv()
            own[core, part] = collect(own[core, part], core, part)
            other[part] = collect(other[part], 1 - core, part)
        put(core, own[core, 0], own[core, 1])
        put(1 - core, other[0], other[1])

    for rel in range(4):

        @pl.when(z != chips[rel])
        def _():
            for side in range(pairs):
                for part in (0, 1):
                    send(rel, side, part).wait_send()

    for chunk in range(CHUNKS):
        near(0, chunk).wait_send()
        near(1, chunk).wait_send()
        forward(chunk).wait_send()
    for part in (0, 1):
        share(part).wait_send()
    for copy in amp_shares:
        copy.wait_send()


def fused(nz, slots, pairs, number, amplitudes, packed, occ_irrep, vir_irrep, energies):
    rows, depth = amplitudes.shape
    k_tiles = depth // TILE
    vmem = pl.BlockSpec(memory_space=pltpu.VMEM)
    hbm = pl.BlockSpec(memory_space=pltpu.HBM)
    dma = pltpu.SemaphoreType.DMA
    return pl.pallas_call(
        functools.partial(cycle_kernel, nz, slots, pairs),
        out_shape=jax.ShapeDtypeStruct((rows, TILE), jnp.float32),
        in_specs=[hbm, vmem, vmem, vmem, vmem],
        out_specs=vmem,
        scratch_shapes=[
            pltpu.SMEM(occ_irrep.shape, jnp.int32),
            pltpu.SMEM(vir_irrep.shape, jnp.int32),
            pltpu.SMEM((4 * pairs * slots,), jnp.int32),
            pltpu.VMEM((4, 2, slots * HALF, COLS), jnp.bfloat16),
            pltpu.VMEM((2 * k_tiles + 1, rows, TILE), jnp.bfloat16),
            pltpu.VMEM((pairs, 2, HALF, COLS), jnp.float32),
            pltpu.VMEM((4, pairs, 2, CODE_ROWS, COLS), jnp.int16),
            pltpu.VMEM((nz, pairs, 2, CODE_ROWS, COLS), jnp.int16),
            pltpu.VMEM((2, HALF, COLS), jnp.float32),
            pltpu.VMEM((rows, TILE), jnp.float32),
            dma((3,)),
            dma((3, k_tiles)),
            dma((2, CHUNKS)),
            dma((3, CHUNKS)),
            dma((CHUNKS,)),
            dma((4, pairs, 2)),
            dma((nz, pairs, 2)),
            dma((2, 2)),
        ],
        compiler_params=pltpu.CompilerParams(
            collective_id=number, has_side_effects=True, vmem_limit_bytes=40 << 20
        ),
    )(amplitudes, packed, occ_irrep, vir_irrep, energies)


def choice_kernel(
    nz,
    k_tiles,
    rows,
    int_hbm,
    occ_irr_hbm,
    vir_irr_hbm,
    occ_e_hbm,
    vir_e_hbm,
    choice,
    packed,
    occ_irr_out,
    vir_irr_out,
    energies,
    mine,
    occ_irr,
    vir_irr,
    occ_e,
    int_sem,
    small_sem,
):
    r = lax.axis_index("row")
    z = lax.axis_index("col")
    tiles_virtual = vir_irr.shape[0]
    half = TILE // 2
    irr_copies = [
        pltpu.make_async_copy(occ_irr_hbm, occ_irr, small_sem.at[0]),
        pltpu.make_async_copy(vir_irr_hbm, vir_irr, small_sem.at[1]),
    ]
    other_copies = [
        pltpu.make_async_copy(occ_irr_hbm, occ_irr_out, small_sem.at[2]),
        pltpu.make_async_copy(vir_irr_hbm, vir_irr_out, small_sem.at[3]),
        pltpu.make_async_copy(occ_e_hbm, occ_e, small_sem.at[4]),
    ]
    for i in range(4):
        tile = (r if i < 2 else z) % tiles_virtual
        start = pl.multiple_of(tile * TILE + (i % 2) * half, half)
        other_copies.append(
            pltpu.make_async_copy(
                vir_e_hbm.at[pl.ds(start, half)], energies.at[i], small_sem.at[5 + i]
            )
        )
    int_copies = []
    for tile in range(k_tiles):
        here = pl.ds(tile * TILE, TILE)
        int_copies.append(
            pltpu.make_async_copy(int_hbm.at[here], mine.at[tile], int_sem.at[tile])
        )
    for copy in (*irr_copies, *int_copies, *other_copies):
        copy.start()
    for copy in irr_copies:
        copy.wait()

    def irrep(number):
        return occ_irr[number // tiles_virtual] ^ vir_irr[number % tiles_virtual]

    chosen = select_tiles(
        [irrep(z * k_tiles + tile) for tile in range(k_tiles)], irrep(r // 2), k_tiles
    )
    q_irr = [irrep(number) for number in range(nz)]
    worst = jnp.int32(0)
    for part in range(nz):
        k_irr = [irrep(part * k_tiles + tile) for tile in range(k_tiles)]
        for q in range(nz):
            count = jnp.int32(0)
            for tile in range(k_tiles):
                count = count + jnp.where(k_irr[tile] == q_irr[q], 1, 0)
            worst = jnp.maximum(worst, count)
    which = jnp.int32(0)
    for slots in SLOTS:
        which = which + jnp.where(worst > slots, 1, 0)
    both = jnp.int32(0)
    for row in range(0, rows, 2):
        first = irrep(row)
        wanted = jnp.int32(0)
        for q in range(nz):
            wanted = wanted + jnp.where(q_irr[q] == first, 1, 0)
        clash = jnp.logical_and(irrep(row + 1) == first, wanted > 0)
        both = jnp.where(clash, 1, both)
    choice[0] = which + both * (len(SLOTS) + 1)

    for copy in int_copies:
        copy.wait()
    mid = COLS // 2
    for number, slots in enumerate((*SLOTS, k_tiles)):

        @pl.when(which == number)
        def _():
            parts = []
            for s in range(slots):
                tile = mine[jnp.minimum(chosen[s], k_tiles - 1)]
                parts += [tile[:HALF], tile[HALF:]]
            for i in range(slots):
                one, two = parts[i], parts[i + slots]
                here = pl.ds(i * HALF, HALF)
                packed[0, here] = jnp.concatenate([one[:, :mid], two[:, :mid]], axis=1)
                packed[1, here] = jnp.concatenate([one[:, mid:], two[:, mid:]], axis=1)

    for copy in other_copies:
        copy.wait()
    row_occ = occ_e[r // tiles_virtual]
    col_occ = occ_e[z // tiles_virtual]
    energies[0:2] = energies[0:2] - row_occ
    energies[2:4] = energies[2:4] - col_occ


def block_sparse(nz, rows, amplitudes, integrals, occ_irrep, vir_irrep, occ_energy, vir_energy):
    k_tiles = amplitudes.shape[1] // TILE
    smem = pl.BlockSpec(memory_space=pltpu.SMEM)
    vmem = pl.BlockSpec(memory_space=pltpu.VMEM)
    hbm = pl.BlockSpec(memory_space=pltpu.HBM)
    dma = pltpu.SemaphoreType.DMA
    choice, *rest = pl.pallas_call(
        functools.partial(choice_kernel, nz, k_tiles, rows),
        out_shape=[
            jax.ShapeDtypeStruct((1,), jnp.int32),
            jax.ShapeDtypeStruct((2, k_tiles * HALF, COLS), integrals.dtype),
            jax.ShapeDtypeStruct(occ_irrep.shape, jnp.int32),
            jax.ShapeDtypeStruct(vir_irrep.shape, jnp.int32),
            jax.ShapeDtypeStruct((4, TILE // 2), jnp.float32),
        ],
        in_specs=[hbm] * 5,
        out_specs=[smem, vmem, vmem, vmem, vmem],
        scratch_shapes=[
            pltpu.VMEM((k_tiles, TILE, COLS), jnp.bfloat16),
            pltpu.SMEM(occ_irrep.shape, jnp.int32),
            pltpu.SMEM(vir_irrep.shape, jnp.int32),
            pltpu.SMEM(occ_energy.shape, jnp.float32),
            dma((k_tiles,)),
            dma((9,)),
        ],
    )(integrals, occ_irrep, vir_irrep, occ_energy, vir_energy)
    kinds = [(slots, pairs) for pairs in (1, 2) for slots in (*SLOTS, k_tiles)]
    branches = [
        functools.partial(fused, nz, slots, pairs, number)
        for number, (slots, pairs) in enumerate(kinds)
    ]
    return lax.switch(choice[0], branches, amplitudes, *rest)


def solution(mesh):
    row, col = mesh.shape["row"], mesh.shape["col"]

    def shards(amplitudes, integrals, occ_irrep, vir_irrep, occ_energy, vir_energy):
        args = (amplitudes, integrals, occ_irrep, vir_irrep, occ_energy, vir_energy)
        plain = (
            (row, col) == (8, 4)
            and amplitudes.shape[0] == TILE
            and integrals.shape[1] == COLS
            and vir_energy.shape[0] == TILE * vir_irrep.shape[0]
        )
        return block_sparse(col, row, *args) if plain else general(*args)

    return jax.shard_map(
        shards,
        mesh=mesh,
        in_specs=(P("row", "col"), P("col", "row"), P(), P(), P(), P()),
        out_specs=P("row", "col"),
        check_vma=False,
    )
```

```python
import functools

import jax
import jax.numpy as jnp
from jax import lax
from jax.experimental import pallas as pl
from jax.experimental.pallas import tpu as pltpu
from jax.sharding import PartitionSpec as P

TILE = 256
MESH = pl.DeviceIdType.MESH


def lookup(table, index):
    hits = index[:, None] == jnp.arange(table.shape[0], dtype=jnp.int32)[None, :]
    return jnp.sum(jnp.where(hits, table[None, :], jnp.zeros_like(table)[None, :]), axis=1)


def irreps(first_tile, count, occ_irrep, vir_irrep, tiles_virtual):
    tiles = first_tile + jnp.arange(count, dtype=jnp.int32)
    return jnp.bitwise_xor(
        lookup(occ_irrep, tiles // tiles_virtual), lookup(vir_irrep, tiles % tiles_virtual)
    )


def general(amplitudes, integrals, occ_irrep, vir_irrep, occ_energy, vir_energy):
    tile_size = TILE
    tiles_virtual = vir_irrep.shape[0]
    virtual_count = vir_energy.shape[0]
    p_rows, k_cols = amplitudes.shape
    p_tiles = p_rows // tile_size
    k_tiles = k_cols // tile_size
    row_index = lax.axis_index("row")
    col_index = lax.axis_index("col")
    p_irr = irreps(row_index * p_tiles, p_tiles, occ_irrep, vir_irrep, tiles_virtual)
    k_irr = irreps(col_index * k_tiles, k_tiles, occ_irrep, vir_irrep, tiles_virtual)
    match = p_irr[:, None] == k_irr[None, :]
    masked_amp = (
        amplitudes.reshape(p_tiles, tile_size, k_tiles, tile_size)
        * match[:, None, :, None].astype(jnp.bfloat16)
    ).reshape(p_rows, k_cols)
    piece = lax.all_gather(integrals, "row", axis=1, tiled=True)
    width = piece.shape[1]
    columns = jnp.arange(width, dtype=jnp.int32)
    column_tiles = columns // tile_size
    q_irr = jnp.bitwise_xor(
        lookup(occ_irrep, column_tiles // tiles_virtual),
        lookup(vir_irrep, column_tiles % tiles_virtual),
    )
    keeper = (k_irr[:, None] == q_irr[None, :]).astype(jnp.bfloat16)
    masked_int = (piece.reshape(k_tiles, tile_size, width) * keeper[:, None, :]).reshape(
        k_cols, width
    )
    partial_cycle = jnp.dot(masked_amp, masked_int, preferred_element_type=jnp.float32)
    cycle = lax.psum_scatter(partial_cycle, "col", scatter_dimension=1, tiled=True)
    q_cols = cycle.shape[1]
    row_pairs = row_index * p_rows + jnp.arange(p_rows, dtype=jnp.int32)
    col_pairs = col_index * q_cols + jnp.arange(q_cols, dtype=jnp.int32)
    row_energy = lookup(vir_energy, row_pairs % virtual_count) - lookup(
        occ_energy, row_pairs // virtual_count
    )
    col_energy = lookup(vir_energy, col_pairs % virtual_count) - lookup(
        occ_energy, col_pairs // virtual_count
    )
    return cycle / (row_energy[:, None] + col_energy[None, :])


CHUNKS = 4
COLS = 128
SLOTS = (3, 4, 5)
TOP = 32767.0
HALF = TILE // 2
CODE_ROWS = HALF + 16


def select_tiles(k_irr, irrep, slots):
    tiles = len(k_irr)
    found = [jnp.int32(tiles)] * slots
    count = jnp.int32(0)
    for tile in range(tiles):
        hit = k_irr[tile] == irrep
        found = [
            jnp.where(jnp.logical_and(hit, count == s), tile, found[s]) for s in range(slots)
        ]
        count = count + jnp.where(hit, 1, 0)
    return found


def cycle_kernel(
    nz,
    slots,
    pairs,
    amp_hbm,
    packed,
    occ_irr_in,
    vir_irr_in,
    energies,
    out_ref,
    occ_irr,
    vir_irr,
    table,
    blocks,
    amp,
    own,
    codes,
    in_codes,
    other,
    inverse,
    small_sem,
    amp_sem,
    near_send,
    near_recv,
    fwd_send,
    z_send,
    z_recv,
    last_sem,
):
    r = lax.axis_index("row")
    z = lax.axis_index("col")
    core = r % 2
    chip = r // 2
    x = chip % 2
    y = chip // 2
    chip_x = chip + 1 - 2 * x
    chip_y = chip + 2 - 4 * y
    chips = (chip, chip_x, chip_y, chip_x + chip_y - chip)
    xr = 2 * chip_x + core
    yr = 2 * chip_y + core
    sr = r + 1 - 2 * core
    tiles_virtual = vir_irr.shape[0]
    k_tiles = amp_hbm.shape[1] // TILE
    zero_tile = 2 * k_tiles
    depth = slots * HALF
    step = depth // 2

    def remote(src, dst, send_sem, recv_sem, target):
        return pltpu.make_async_remote_copy(
            src_ref=src,
            dst_ref=dst,
            send_sem=send_sem,
            recv_sem=recv_sem,
            device_id=target,
            device_id_type=MESH,
        )

    irr_copies = [
        pltpu.make_async_copy(occ_irr_in, occ_irr, small_sem.at[0]),
        pltpu.make_async_copy(vir_irr_in, vir_irr, small_sem.at[1]),
    ]
    amp_copies = []
    amp_shares = []
    for tile in range(k_tiles):
        here = pl.ds(tile * TILE, TILE)
        place = amp.at[core * k_tiles + tile]
        amp_copies.append(
            pltpu.make_async_copy(amp_hbm.at[:, here], place, amp_sem.at[0, tile])
        )
        amp_shares.append(
            remote(
                amp_hbm.at[:, here], place, amp_sem.at[1, tile], amp_sem.at[2, tile], (sr, z)
            )
        )
    own_copy = pltpu.make_async_copy(
        packed.at[:, pl.ds(0, depth)], blocks.at[chip], small_sem.at[2]
    )
    for copy in (*irr_copies, *amp_copies, own_copy):
        copy.start()

    barrier = pltpu.get_barrier_semaphore()
    for target in (xr, yr, sr):
        pl.semaphore_signal(barrier, inc=1, device_id=(target, z), device_id_type=MESH)
    rows_met = (r,) if pairs == 1 else (r, sr)
    for k in range(1, nz):
        for row in rows_met:
            pl.semaphore_signal(
                barrier, inc=1, device_id=(row, (z + k) % nz), device_id_type=MESH
            )

    pl.semaphore_wait(barrier, 3 + len(rows_met) * (nz - 1))

    x_order = (0, 1, 2, 3)
    y_order = (1, 0, 3, 2)

    def piece(source, chunk):
        return blocks.at[source, chunk // 2, pl.ds(chunk % 2 * step, step)]

    def near(axis, chunk):
        return remote(
            packed.at[chunk // 2, pl.ds(chunk % 2 * step, step)],
            piece(chip, chunk),
            near_send.at[axis, chunk],
            near_recv.at[axis, chunk],
            ((xr, yr)[axis], z),
        )

    def arrival(rel, chunk):
        ref = piece(chips[rel], chunk)
        return remote(ref, ref, near_send.at[0, chunk], near_recv.at[rel - 1, chunk], (xr, z))

    def forward(chunk):
        source, target = (chip_x, yr) if chunk % 2 == 0 else (chip_y, xr)
        ref = piece(source, chunk)
        return remote(ref, ref, fwd_send.at[chunk], near_recv.at[2, chunk], (target, z))

    for cx, cy in zip(x_order[:3], y_order[:3]):
        near(0, cx).start()
        near(1, cy).start()

    for copy in amp_shares:
        copy.start()
    amp[zero_tile] = jnp.zeros((TILE, TILE), jnp.bfloat16)

    for copy in irr_copies:
        copy.wait()

    def irrep(number):
        return occ_irr[number // tiles_virtual] ^ vir_irr[number % tiles_virtual]

    k_irr = [irrep(z * k_tiles + tile) for tile in range(k_tiles)]
    q_irr = [irrep(source) for source in chips]
    first_irr = irrep(2 * chip)
    for rel in range(4):
        chosen = select_tiles(k_irr, q_irr[rel], slots)
        for side in range(pairs):
            row = side if pairs == 2 else jnp.where(first_irr == q_irr[rel], 0, 1)
            for i, tile in enumerate(chosen):
                table[(rel * pairs + side) * slots + i] = jnp.where(
                    tile == k_tiles, zero_tile, row * k_tiles + tile
                )
    own_copy.wait()

    low = lax.broadcasted_iota(jnp.int32, (HALF, COLS), 1) < COLS // 2

    def swap(values):
        return pltpu.roll(values, COLS // 2, 1)

    def chip_of(rel):
        return (x + rel % 2) % 2 + 2 * ((y + rel // 2) % 2)

    def send(rel, side, part):
        place = 0 if pairs == 1 else core
        row = r if pairs == 1 else 2 * chip + side
        return remote(
            codes.at[rel, side, part],
            in_codes.at[z, place, part],
            z_send.at[rel, side, part],
            z_recv.at[z, place, part],
            (row, chip_of(rel)),
        )

    def share(part):
        given = 0 if pairs == 1 else 1 - core
        return remote(
            own.at[given, part], other.at[part], last_sem.at[0, part], last_sem.at[1, part], (sr, z)
        )

    def multiply(rel, side, part):
        source = chip_of(rel)
        left = jnp.concatenate(
            [amp[table[(rel * pairs + side) * slots + i]] for i in range(slots)], axis=1
        )
        right = blocks[source, part]
        one = jnp.dot(left[:, :depth], right, preferred_element_type=jnp.float32)
        two = jnp.dot(left[:, depth:], right, preferred_element_type=jnp.float32)
        product = jnp.where(
            low, one[:HALF] + swap(two[:HALF]), swap(one[HALF:]) + two[HALF:]
        )

        @pl.when(z == source)
        def _():
            own[side, part] = product

        @pl.when(z != source)
        def _():
            groups = product.reshape(HALF // 16, 16, COLS)
            most = jnp.maximum(jnp.max(jnp.abs(groups), axis=0), 1e-30)
            power = jnp.ceil(jnp.log2(most))
            scaled = jnp.floor(groups * (TOP * jnp.exp2(-power))[None] + 0.5)
            ints = jnp.clip(scaled, -TOP, TOP).astype(jnp.int32)
            codes[rel, side, part, pl.ds(0, HALF)] = ints.reshape(HALF, COLS).astype(jnp.int16)
            codes[rel, side, part, pl.ds(HALF, 16)] = power.astype(jnp.int32).astype(jnp.int16)
            send(rel, side, part).start()

    def pass_on(*chunks):
        for chunk in chunks:
            arrival(1 + chunk % 2, chunk).wait_recv()
            forward(chunk).start()

    def when(turn, number):
        return pl.when(turn == number)

    def turn_body(turn, _):
        rel = jnp.where(turn < 2, 0, (turn + 1) % 3 + 1)
        part = jnp.where(turn < 2, turn, (turn + 1) // 3 - 1)

        @when(turn, 2)
        def _():
            arrival(1, 1).wait_recv()

        @when(turn, 3)
        def _():
            arrival(2, 0).wait_recv()

        @when(turn, 4)
        def _():
            pass_on(2, 3)
            arrival(3, 0).wait_recv()
            arrival(3, 1).wait_recv()

        @when(turn, 5)
        def _():
            row_energy = jnp.concatenate([energies[0:1], energies[1:2]], axis=1)
            col_energy = jnp.concatenate([energies[2:3], energies[3:4]], axis=1)
            keep = jnp.where(irrep(r) == irrep(z), 1.0, 0.0).astype(jnp.float32)
            inverse[...] = keep / (jnp.broadcast_to(row_energy, (TILE, TILE)).T + col_energy)
            arrival(1, 3).wait_recv()

        @when(turn, 6)
        def _():
            arrival(2, 2).wait_recv()

        @when(turn, 7)
        def _():
            arrival(3, 2).wait_recv()
            arrival(3, 3).wait_recv()

        for side in range(pairs):
            multiply(rel, side, part)
        if pairs == 2:

            @pl.when(z == chip_of(rel))
            def _():
                share(part).start()

        return 0

    pass_on(0, 1)
    near(0, x_order[3]).start()
    near(1, y_order[3]).start()
    for copy in amp_copies:
        copy.wait()
    for copy in amp_shares:
        copy.wait_recv()
    lax.fori_loop(0, 8, turn_body, 0)

    def collect(total, place, part):
        for k in range(1, nz):
            source = (z + k) % nz
            ref = in_codes.at[source, place, part]
            remote(
                ref, ref, z_send.at[0, 0, part], z_recv.at[source, place, part], (r, source)
            ).wait_recv()
            values = in_codes[source, place, part, pl.ds(0, HALF)].astype(jnp.int32)
            values = values.astype(jnp.float32).reshape(HALF // 16, 16, COLS)
            powers = in_codes[source, place, part, pl.ds(HALF, 16)].astype(jnp.int32)
            scale = jnp.exp2(powers.astype(jnp.float32)) * (1.0 / TOP)
            total = total + (values * scale[None]).reshape(HALF, COLS)
        return total

    def put(half_core, first, last):
        here = pl.ds(pl.multiple_of(half_core * COLS, COLS), COLS)
        top = jnp.where(low, first, swap(last))
        bottom = jnp.where(low, swap(first), last)
        out_ref[:HALF, here] = top * inverse[:HALF, here]
        out_ref[HALF:, here] = bottom * inverse[HALF:, here]

    if pairs == 1:
        for part in (0, 1):
            own[0, part] = collect(own[0, part], 0, part)
            share(part).start()
        put(core, own[0, 0], own[0, 1])
        for part in (0, 1):
            share(part).wait_recv()
        put(1 - core, other[0], other[1])
    else:
        for part in (0, 1):
            share(part).wait_recv()
            own[core, part] = collect(own[core, part], core, part)
            other[part] = collect(other[part], 1 - core, part)
        put(core, own[core, 0], own[core, 1])
        put(1 - core, other[0], other[1])

    for rel in range(4):

        @pl.when(z != chips[rel])
        def _():
            for side in range(pairs):
                for part in (0, 1):
                    send(rel, side, part).wait_send()

    for chunk in range(CHUNKS):
        near(0, chunk).wait_send()
        near(1, chunk).wait_send()
        forward(chunk).wait_send()
    for part in (0, 1):
        share(part).wait_send()
    for copy in amp_shares:
        copy.wait_send()


def fused(nz, slots, pairs, number, amplitudes, packed, occ_irrep, vir_irrep, energies):
    rows, depth = amplitudes.shape
    k_tiles = depth // TILE
    vmem = pl.BlockSpec(memory_space=pltpu.VMEM)
    hbm = pl.BlockSpec(memory_space=pltpu.HBM)
    dma = pltpu.SemaphoreType.DMA
    return pl.pallas_call(
        functools.partial(cycle_kernel, nz, slots, pairs),
        out_shape=jax.ShapeDtypeStruct((rows, TILE), jnp.float32),
        in_specs=[hbm, vmem, vmem, vmem, vmem],
        out_specs=vmem,
        scratch_shapes=[
            pltpu.SMEM(occ_irrep.shape, jnp.int32),
            pltpu.SMEM(vir_irrep.shape, jnp.int32),
            pltpu.SMEM((4 * pairs * slots,), jnp.int32),
            pltpu.VMEM((4, 2, slots * HALF, COLS), jnp.bfloat16),
            pltpu.VMEM((2 * k_tiles + 1, rows, TILE), jnp.bfloat16),
            pltpu.VMEM((pairs, 2, HALF, COLS), jnp.float32),
            pltpu.VMEM((4, pairs, 2, CODE_ROWS, COLS), jnp.int16),
            pltpu.VMEM((nz, pairs, 2, CODE_ROWS, COLS), jnp.int16),
            pltpu.VMEM((2, HALF, COLS), jnp.float32),
            pltpu.VMEM((rows, TILE), jnp.float32),
            dma((3,)),
            dma((3, k_tiles)),
            dma((2, CHUNKS)),
            dma((3, CHUNKS)),
            dma((CHUNKS,)),
            dma((4, pairs, 2)),
            dma((nz, pairs, 2)),
            dma((2, 2)),
        ],
        compiler_params=pltpu.CompilerParams(
            collective_id=number, has_side_effects=True, vmem_limit_bytes=40 << 20
        ),
    )(amplitudes, packed, occ_irrep, vir_irrep, energies)


def choice_kernel(
    nz,
    k_tiles,
    rows,
    int_hbm,
    occ_irr_hbm,
    vir_irr_hbm,
    occ_e_hbm,
    vir_e_hbm,
    choice,
    packed,
    occ_irr_out,
    vir_irr_out,
    energies,
    mine,
    occ_irr,
    vir_irr,
    occ_e,
    found,
    picked,
    int_sem,
    small_sem,
):
    r = lax.axis_index("row")
    z = lax.axis_index("col")
    tiles_virtual = vir_irr.shape[0]
    half = TILE // 2
    irr_copies = [
        pltpu.make_async_copy(occ_irr_hbm, occ_irr, small_sem.at[0]),
        pltpu.make_async_copy(vir_irr_hbm, vir_irr, small_sem.at[1]),
    ]
    other_copies = [
        pltpu.make_async_copy(occ_irr_hbm, occ_irr_out, small_sem.at[2]),
        pltpu.make_async_copy(vir_irr_hbm, vir_irr_out, small_sem.at[3]),
        pltpu.make_async_copy(occ_e_hbm, occ_e, small_sem.at[4]),
    ]
    for i in range(4):
        tile = (r if i < 2 else z) % tiles_virtual
        start = pl.multiple_of(tile * TILE + (i % 2) * half, half)
        other_copies.append(
            pltpu.make_async_copy(
                vir_e_hbm.at[pl.ds(start, half)], energies.at[i], small_sem.at[5 + i]
            )
        )
    int_copies = []
    for tile in range(k_tiles):
        here = pl.ds(tile * TILE, TILE)
        int_copies.append(
            pltpu.make_async_copy(int_hbm.at[here], mine.at[tile], int_sem.at[tile])
        )
    for copy in (*irr_copies, *int_copies, *other_copies):
        copy.start()
    for copy in irr_copies:
        copy.wait()

    def irrep(number):
        return occ_irr[number // tiles_virtual] ^ vir_irr[number % tiles_virtual]

    def count_up(counts, number):
        return counts + lax.shift_left(jnp.int32(1), 8 * irrep(number))

    def count_of(counts, value):
        return lax.shift_right_logical(counts, 8 * value) & 255

    q_irr = [irrep(number) for number in range(nz)]
    worst = jnp.int32(0)
    for part in range(nz):
        counts = jnp.int32(0)
        for tile in range(k_tiles):
            counts = count_up(counts, part * k_tiles + tile)
        for value in q_irr:
            worst = jnp.maximum(worst, count_of(counts, value))
    which = jnp.int32(0)
    for slots in SLOTS:
        which = which + jnp.where(worst > slots, 1, 0)
    wanted = jnp.int32(0)
    for number in range(nz):
        wanted = count_up(wanted, number)
    both = jnp.int32(0)
    for row in range(0, rows, 2):
        first = irrep(row)
        clash = jnp.logical_and(irrep(row + 1) == first, count_of(wanted, first) > 0)
        both = jnp.where(clash, 1, both)
    picked[0] = which + both * (len(SLOTS) + 1)
    choice_copy = pltpu.make_async_copy(picked, choice, small_sem.at[9])
    choice_copy.start()

    for s in range(k_tiles):
        found[s] = 0
    mine_irr = irrep(r // 2)
    place = jnp.int32(0)
    for tile in range(k_tiles):
        found[place] = tile
        place = place + jnp.where(irrep(z * k_tiles + tile) == mine_irr, 1, 0)
    chosen = [found[s] for s in range(k_tiles)]

    for copy in int_copies:
        copy.wait()
    mid = COLS // 2
    for number, slots in enumerate((*SLOTS, k_tiles)):

        @pl.when(which == number)
        def _():
            parts = []
            for s in range(slots):
                tile = mine[chosen[s]]
                parts += [tile[:HALF], tile[HALF:]]
            for i in range(slots):
                one, two = parts[i], parts[i + slots]
                here = pl.ds(i * HALF, HALF)
                packed[0, here] = jnp.concatenate([one[:, :mid], two[:, :mid]], axis=1)
                packed[1, here] = jnp.concatenate([one[:, mid:], two[:, mid:]], axis=1)

    for copy in other_copies:
        copy.wait()
    row_occ = occ_e[r // tiles_virtual]
    col_occ = occ_e[z // tiles_virtual]
    energies[0:2] = energies[0:2] - row_occ
    energies[2:4] = energies[2:4] - col_occ
    choice_copy.wait()


def block_sparse(nz, rows, amplitudes, integrals, occ_irrep, vir_irrep, occ_energy, vir_energy):
    k_tiles = amplitudes.shape[1] // TILE
    vmem = pl.BlockSpec(memory_space=pltpu.VMEM)
    hbm = pl.BlockSpec(memory_space=pltpu.HBM)
    dma = pltpu.SemaphoreType.DMA
    choice, *rest = pl.pallas_call(
        functools.partial(choice_kernel, nz, k_tiles, rows),
        out_shape=[
            jax.ShapeDtypeStruct((1,), jnp.int32),
            jax.ShapeDtypeStruct((2, k_tiles * HALF, COLS), integrals.dtype),
            jax.ShapeDtypeStruct(occ_irrep.shape, jnp.int32),
            jax.ShapeDtypeStruct(vir_irrep.shape, jnp.int32),
            jax.ShapeDtypeStruct((4, TILE // 2), jnp.float32),
        ],
        in_specs=[hbm] * 5,
        out_specs=[hbm, vmem, vmem, vmem, vmem],
        scratch_shapes=[
            pltpu.VMEM((k_tiles, TILE, COLS), jnp.bfloat16),
            pltpu.SMEM(occ_irrep.shape, jnp.int32),
            pltpu.SMEM(vir_irrep.shape, jnp.int32),
            pltpu.SMEM(occ_energy.shape, jnp.float32),
            pltpu.SMEM((k_tiles,), jnp.int32),
            pltpu.SMEM((1,), jnp.int32),
            dma((k_tiles,)),
            dma((10,)),
        ],
    )(integrals, occ_irrep, vir_irrep, occ_energy, vir_energy)
    kinds = [(slots, pairs) for pairs in (1, 2) for slots in (*SLOTS, k_tiles)]
    branches = [
        functools.partial(fused, nz, slots, pairs, number)
        for number, (slots, pairs) in enumerate(kinds)
    ]
    return lax.switch(choice[0], branches, amplitudes, *rest)


def solution(mesh):
    row, col = mesh.shape["row"], mesh.shape["col"]

    def shards(amplitudes, integrals, occ_irrep, vir_irrep, occ_energy, vir_energy):
        args = (amplitudes, integrals, occ_irrep, vir_irrep, occ_energy, vir_energy)
        plain = (
            (row, col) == (8, 4)
            and amplitudes.shape[0] == TILE
            and integrals.shape[1] == COLS
            and vir_energy.shape[0] == TILE * vir_irrep.shape[0]
        )
        return block_sparse(col, row, *args) if plain else general(*args)

    return jax.shard_map(
        shards,
        mesh=mesh,
        in_specs=(P("row", "col"), P("col", "row"), P(), P(), P(), P()),
        out_specs=P("row", "col"),
        check_vma=False,
    )
```

```python
import functools

import jax
import jax.numpy as jnp
from jax import lax
from jax.experimental import pallas as pl
from jax.experimental.pallas import tpu as pltpu
from jax.sharding import PartitionSpec as P

TILE = 256
MESH = pl.DeviceIdType.MESH


def lookup(table, index):
    hits = index[:, None] == jnp.arange(table.shape[0], dtype=jnp.int32)[None, :]
    return jnp.sum(jnp.where(hits, table[None, :], jnp.zeros_like(table)[None, :]), axis=1)


def irreps(first_tile, count, occ_irrep, vir_irrep, tiles_virtual):
    tiles = first_tile + jnp.arange(count, dtype=jnp.int32)
    return jnp.bitwise_xor(
        lookup(occ_irrep, tiles // tiles_virtual), lookup(vir_irrep, tiles % tiles_virtual)
    )


def general(amplitudes, integrals, occ_irrep, vir_irrep, occ_energy, vir_energy):
    tile_size = TILE
    tiles_virtual = vir_irrep.shape[0]
    virtual_count = vir_energy.shape[0]
    p_rows, k_cols = amplitudes.shape
    p_tiles = p_rows // tile_size
    k_tiles = k_cols // tile_size
    row_index = lax.axis_index("row")
    col_index = lax.axis_index("col")
    p_irr = irreps(row_index * p_tiles, p_tiles, occ_irrep, vir_irrep, tiles_virtual)
    k_irr = irreps(col_index * k_tiles, k_tiles, occ_irrep, vir_irrep, tiles_virtual)
    match = p_irr[:, None] == k_irr[None, :]
    masked_amp = (
        amplitudes.reshape(p_tiles, tile_size, k_tiles, tile_size)
        * match[:, None, :, None].astype(jnp.bfloat16)
    ).reshape(p_rows, k_cols)
    piece = lax.all_gather(integrals, "row", axis=1, tiled=True)
    width = piece.shape[1]
    columns = jnp.arange(width, dtype=jnp.int32)
    column_tiles = columns // tile_size
    q_irr = jnp.bitwise_xor(
        lookup(occ_irrep, column_tiles // tiles_virtual),
        lookup(vir_irrep, column_tiles % tiles_virtual),
    )
    keeper = (k_irr[:, None] == q_irr[None, :]).astype(jnp.bfloat16)
    masked_int = (piece.reshape(k_tiles, tile_size, width) * keeper[:, None, :]).reshape(
        k_cols, width
    )
    partial_cycle = jnp.dot(masked_amp, masked_int, preferred_element_type=jnp.float32)
    cycle = lax.psum_scatter(partial_cycle, "col", scatter_dimension=1, tiled=True)
    q_cols = cycle.shape[1]
    row_pairs = row_index * p_rows + jnp.arange(p_rows, dtype=jnp.int32)
    col_pairs = col_index * q_cols + jnp.arange(q_cols, dtype=jnp.int32)
    row_energy = lookup(vir_energy, row_pairs % virtual_count) - lookup(
        occ_energy, row_pairs // virtual_count
    )
    col_energy = lookup(vir_energy, col_pairs % virtual_count) - lookup(
        occ_energy, col_pairs // virtual_count
    )
    return cycle / (row_energy[:, None] + col_energy[None, :])


CHUNKS = 4
COLS = 128
SLOTS = (3, 4, 5)
TOP = 32767.0
HALF = TILE // 2
CODE_ROWS = HALF + 16


def select_tiles(k_irr, irrep, slots):
    tiles = len(k_irr)
    found = [jnp.int32(tiles)] * slots
    count = jnp.int32(0)
    for tile in range(tiles):
        hit = k_irr[tile] == irrep
        found = [
            jnp.where(jnp.logical_and(hit, count == s), tile, found[s]) for s in range(slots)
        ]
        count = count + jnp.where(hit, 1, 0)
    return found


def cycle_kernel(
    nz,
    slots,
    pairs,
    amp_hbm,
    packed,
    occ_irr_in,
    vir_irr_in,
    energies,
    out_ref,
    occ_irr,
    vir_irr,
    table,
    blocks,
    amp,
    own,
    codes,
    in_codes,
    powers,
    other,
    inverse,
    small_sem,
    amp_sem,
    near_send,
    near_recv,
    fwd_send,
    z_send,
    z_recv,
    last_sem,
):
    r = lax.axis_index("row")
    z = lax.axis_index("col")
    core = r % 2
    chip = r // 2
    x = chip % 2
    y = chip // 2
    chip_x = chip + 1 - 2 * x
    chip_y = chip + 2 - 4 * y
    chips = (chip, chip_x, chip_y, chip_x + chip_y - chip)
    xr = 2 * chip_x + core
    yr = 2 * chip_y + core
    sr = r + 1 - 2 * core
    tiles_virtual = vir_irr.shape[0]
    k_tiles = amp_hbm.shape[1] // TILE
    zero_tile = 2 * k_tiles
    depth = slots * HALF
    step = depth // 2

    def remote(src, dst, send_sem, recv_sem, target):
        return pltpu.make_async_remote_copy(
            src_ref=src,
            dst_ref=dst,
            send_sem=send_sem,
            recv_sem=recv_sem,
            device_id=target,
            device_id_type=MESH,
        )

    barrier = pltpu.get_barrier_semaphore()
    for target in (xr, yr, sr):
        pl.semaphore_signal(barrier, inc=1, device_id=(target, z), device_id_type=MESH)
    rows_met = (r,) if pairs == 1 else (r, sr)
    for k in range(1, nz):
        for row in rows_met:
            pl.semaphore_signal(
                barrier, inc=1, device_id=(row, (z + k) % nz), device_id_type=MESH
            )

    irr_copies = [
        pltpu.make_async_copy(occ_irr_in, occ_irr, small_sem.at[0]),
        pltpu.make_async_copy(vir_irr_in, vir_irr, small_sem.at[1]),
    ]
    amp_copies = []
    amp_shares = []
    for tile in range(k_tiles):
        here = pl.ds(tile * TILE, TILE)
        place = amp.at[core * k_tiles + tile]
        amp_copies.append(
            pltpu.make_async_copy(amp_hbm.at[:, here], place, amp_sem.at[0, tile])
        )
        amp_shares.append(
            remote(
                amp_hbm.at[:, here], place, amp_sem.at[1, tile], amp_sem.at[2, tile], (sr, z)
            )
        )
    own_copy = pltpu.make_async_copy(
        packed.at[:, pl.ds(0, depth)], blocks.at[chip], small_sem.at[2]
    )
    for copy in (*irr_copies, *amp_copies, own_copy):
        copy.start()

    pl.semaphore_wait(barrier, 3 + len(rows_met) * (nz - 1))

    x_order = (0, 1, 2, 3)
    y_order = (1, 0, 3, 2)

    def piece(source, chunk):
        return blocks.at[source, chunk // 2, pl.ds(chunk % 2 * step, step)]

    def near(axis, chunk):
        return remote(
            packed.at[chunk // 2, pl.ds(chunk % 2 * step, step)],
            piece(chip, chunk),
            near_send.at[axis, chunk],
            near_recv.at[axis, chunk],
            ((xr, yr)[axis], z),
        )

    def arrival(rel, chunk):
        ref = piece(chips[rel], chunk)
        return remote(ref, ref, near_send.at[0, chunk], near_recv.at[rel - 1, chunk], (xr, z))

    def forward(chunk):
        source, target = (chip_x, yr) if chunk % 2 == 0 else (chip_y, xr)
        ref = piece(source, chunk)
        return remote(ref, ref, fwd_send.at[chunk], near_recv.at[2, chunk], (target, z))

    for cx, cy in zip(x_order[:3], y_order[:3]):
        near(0, cx).start()
        near(1, cy).start()

    for copy in amp_shares:
        copy.start()
    amp[zero_tile] = jnp.zeros((TILE, TILE), jnp.bfloat16)

    for copy in irr_copies:
        copy.wait()

    def irrep(number):
        return occ_irr[number // tiles_virtual] ^ vir_irr[number % tiles_virtual]

    k_irr = [irrep(z * k_tiles + tile) for tile in range(k_tiles)]
    q_irr = [irrep(source) for source in chips]
    first_irr = irrep(2 * chip)
    for rel in range(4):
        chosen = select_tiles(k_irr, q_irr[rel], slots)
        for side in range(pairs):
            row = side if pairs == 2 else jnp.where(first_irr == q_irr[rel], 0, 1)
            for i, tile in enumerate(chosen):
                table[(rel * pairs + side) * slots + i] = jnp.where(
                    tile == k_tiles, zero_tile, row * k_tiles + tile
                )
    own_copy.wait()

    low = lax.broadcasted_iota(jnp.int32, (HALF, COLS), 1) < COLS // 2

    def swap(values):
        return pltpu.roll(values, COLS // 2, 1)

    def chip_of(rel):
        return (x + rel % 2) % 2 + 2 * ((y + rel // 2) % 2)

    def send(rel, side, part, static_part):
        place = 0 if pairs == 1 else core
        row = r if pairs == 1 else 2 * chip + side
        lines = pl.ds(0, HALF if pairs == 2 and static_part == 0 else CODE_ROWS)
        return remote(
            codes.at[rel, side, part, lines],
            in_codes.at[z, place, part, lines],
            z_send.at[rel, side, part],
            z_recv.at[z, place, part],
            (row, chip_of(rel)),
        )

    def share(part):
        given = 0 if pairs == 1 else 1 - core
        return remote(
            own.at[given, part], other.at[part], last_sem.at[0, part], last_sem.at[1, part], (sr, z)
        )

    def multiply(rel, side, part):
        source = chip_of(rel)
        left = jnp.concatenate(
            [amp[table[(rel * pairs + side) * slots + i]] for i in range(slots)], axis=1
        )
        right = blocks[source, part]
        one = jnp.dot(left[:, :depth], right, preferred_element_type=jnp.float32)
        two = jnp.dot(left[:, depth:], right, preferred_element_type=jnp.float32)
        product = jnp.where(
            low, one[:HALF] + swap(two[:HALF]), swap(one[HALF:]) + two[HALF:]
        )

        @pl.when(z == source)
        def _():
            own[side, part] = product

        @pl.when(z != source)
        def _():
            group = 16 if pairs == 1 else 8
            groups = product.reshape(HALF // group, group, COLS)
            most = jnp.maximum(jnp.max(jnp.abs(groups), axis=0), 1e-30)
            power = jnp.ceil(jnp.log2(most))
            scaled = jnp.floor(groups * (TOP * jnp.exp2(-power))[None] + 0.5)
            ints = jnp.clip(scaled, -TOP, TOP).astype(jnp.int32)
            codes[rel, side, part, pl.ds(0, HALF)] = ints.reshape(HALF, COLS).astype(jnp.int16)
            if pairs == 1:
                codes[rel, side, part, pl.ds(HALF, 16)] = power.astype(jnp.int32).astype(
                    jnp.int16
                )
                send(rel, side, part, None).start()
            else:

                @pl.when(part == 0)
                def _():
                    powers[rel, side] = power
                    send(rel, side, part, 0).start()

                @pl.when(part == 1)
                def _():
                    both = jnp.concatenate([powers[rel, side], power], axis=0)
                    codes[rel, side, part, pl.ds(HALF, 16)] = both.astype(jnp.int32).astype(
                        jnp.int16
                    )
                    send(rel, side, part, 1).start()

    def pass_on(*chunks):
        for chunk in chunks:
            arrival(1 + chunk % 2, chunk).wait_recv()
            forward(chunk).start()

    def when(turn, number):
        return pl.when(turn == number)

    def turn_body(turn, _):
        rel = jnp.where(turn < 2, 0, (turn + 1) % 3 + 1)
        part = jnp.where(turn < 2, turn, (turn + 1) // 3 - 1)

        @when(turn, 2)
        def _():
            arrival(1, 1).wait_recv()

        @when(turn, 3)
        def _():
            arrival(2, 0).wait_recv()

        @when(turn, 4)
        def _():
            pass_on(2, 3)
            arrival(3, 0).wait_recv()
            arrival(3, 1).wait_recv()

        @when(turn, 5)
        def _():
            row_energy = jnp.concatenate([energies[0:1], energies[1:2]], axis=1)
            col_energy = jnp.concatenate([energies[2:3], energies[3:4]], axis=1)
            keep = jnp.where(irrep(r) == irrep(z), 1.0, 0.0).astype(jnp.float32)
            inverse[...] = keep / (jnp.broadcast_to(row_energy, (TILE, TILE)).T + col_energy)
            arrival(1, 3).wait_recv()

        @when(turn, 6)
        def _():
            arrival(2, 2).wait_recv()

        @when(turn, 7)
        def _():
            arrival(3, 2).wait_recv()
            arrival(3, 3).wait_recv()

        for side in range(pairs):
            multiply(rel, side, part)
        if pairs == 2:

            @pl.when(z == chip_of(rel))
            def _():
                share(part).start()

        return 0

    pass_on(0, 1)
    near(0, x_order[3]).start()
    near(1, y_order[3]).start()
    for copy in amp_copies:
        copy.wait()
    for copy in amp_shares:
        copy.wait_recv()
    lax.fori_loop(0, 8, turn_body, 0)

    def arrived(source, place, part):
        lines = pl.ds(0, HALF if pairs == 2 and part == 0 else CODE_ROWS)
        ref = in_codes.at[source, place, part, lines]
        remote(
            ref, ref, z_send.at[0, 0, part], z_recv.at[source, place, part], (r, source)
        ).wait_recv()

    def collect(total, place, part):
        group = 16 if pairs == 1 else 8
        for k in range(1, nz):
            source = (z + k) % nz
            if pairs == 1 or part == 0:
                arrived(source, place, part)
            if pairs == 2 and part == 0:
                arrived(source, place, 1)
            values = in_codes[source, place, part, pl.ds(0, HALF)].astype(jnp.int32)
            values = values.astype(jnp.float32).reshape(HALF // group, group, COLS)
            scale = in_codes[source, place, part if pairs == 1 else 1, pl.ds(HALF, 16)]
            scale = jnp.exp2(scale.astype(jnp.int32).astype(jnp.float32)) * (1.0 / TOP)
            if pairs == 2:
                scale = scale[part * 8 : part * 8 + 8]
            total = total + (values * scale[None]).reshape(HALF, COLS)
        return total

    def put(half_core, first, last):
        here = pl.ds(pl.multiple_of(half_core * COLS, COLS), COLS)
        top = jnp.where(low, first, swap(last))
        bottom = jnp.where(low, swap(first), last)
        out_ref[:HALF, here] = top * inverse[:HALF, here]
        out_ref[HALF:, here] = bottom * inverse[HALF:, here]

    if pairs == 1:
        for part in (0, 1):
            own[0, part] = collect(own[0, part], 0, part)
            share(part).start()
        put(core, own[0, 0], own[0, 1])
        for part in (0, 1):
            share(part).wait_recv()
        put(1 - core, other[0], other[1])
    else:
        for part in (0, 1):
            share(part).wait_recv()
            own[core, part] = collect(own[core, part], core, part)
            other[part] = collect(other[part], 1 - core, part)
        put(core, own[core, 0], own[core, 1])
        put(1 - core, other[0], other[1])

    for rel in range(4):

        @pl.when(z != chips[rel])
        def _():
            for side in range(pairs):
                for part in (0, 1):
                    send(rel, side, part, part).wait_send()

    for chunk in range(CHUNKS):
        near(0, chunk).wait_send()
        near(1, chunk).wait_send()
        forward(chunk).wait_send()
    for part in (0, 1):
        share(part).wait_send()
    for copy in amp_shares:
        copy.wait_send()


def fused(nz, slots, pairs, number, amplitudes, packed, occ_irrep, vir_irrep, energies):
    rows, depth = amplitudes.shape
    k_tiles = depth // TILE
    vmem = pl.BlockSpec(memory_space=pltpu.VMEM)
    hbm = pl.BlockSpec(memory_space=pltpu.HBM)
    dma = pltpu.SemaphoreType.DMA
    return pl.pallas_call(
        functools.partial(cycle_kernel, nz, slots, pairs),
        out_shape=jax.ShapeDtypeStruct((rows, TILE), jnp.float32),
        in_specs=[hbm, vmem, vmem, vmem, vmem],
        out_specs=vmem,
        scratch_shapes=[
            pltpu.SMEM(occ_irrep.shape, jnp.int32),
            pltpu.SMEM(vir_irrep.shape, jnp.int32),
            pltpu.SMEM((4 * pairs * slots,), jnp.int32),
            pltpu.VMEM((4, 2, slots * HALF, COLS), jnp.bfloat16),
            pltpu.VMEM((2 * k_tiles + 1, rows, TILE), jnp.bfloat16),
            pltpu.VMEM((pairs, 2, HALF, COLS), jnp.float32),
            pltpu.VMEM((4, pairs, 2, CODE_ROWS, COLS), jnp.int16),
            pltpu.VMEM((nz, pairs, 2, CODE_ROWS, COLS), jnp.int16),
            pltpu.VMEM((4, 2, 8, COLS), jnp.float32),
            pltpu.VMEM((2, HALF, COLS), jnp.float32),
            pltpu.VMEM((rows, TILE), jnp.float32),
            dma((3,)),
            dma((3, k_tiles)),
            dma((2, CHUNKS)),
            dma((3, CHUNKS)),
            dma((CHUNKS,)),
            dma((4, pairs, 2)),
            dma((nz, pairs, 2)),
            dma((2, 2)),
        ],
        compiler_params=pltpu.CompilerParams(
            collective_id=number, has_side_effects=True, vmem_limit_bytes=40 << 20
        ),
    )(amplitudes, packed, occ_irrep, vir_irrep, energies)


def choice_kernel(
    nz,
    k_tiles,
    rows,
    int_hbm,
    occ_irr_hbm,
    vir_irr_hbm,
    occ_e_hbm,
    vir_e_hbm,
    choice,
    packed,
    occ_irr_out,
    vir_irr_out,
    energies,
    mine,
    occ_irr,
    vir_irr,
    occ_e,
    found,
    picked,
    int_sem,
    small_sem,
):
    r = lax.axis_index("row")
    z = lax.axis_index("col")
    tiles_virtual = vir_irr.shape[0]
    half = TILE // 2
    irr_copies = [
        pltpu.make_async_copy(occ_irr_hbm, occ_irr, small_sem.at[0]),
        pltpu.make_async_copy(vir_irr_hbm, vir_irr, small_sem.at[1]),
    ]
    other_copies = [
        pltpu.make_async_copy(occ_irr_hbm, occ_irr_out, small_sem.at[2]),
        pltpu.make_async_copy(vir_irr_hbm, vir_irr_out, small_sem.at[3]),
        pltpu.make_async_copy(occ_e_hbm, occ_e, small_sem.at[4]),
    ]
    for i in range(4):
        tile = (r if i < 2 else z) % tiles_virtual
        start = pl.multiple_of(tile * TILE + (i % 2) * half, half)
        other_copies.append(
            pltpu.make_async_copy(
                vir_e_hbm.at[pl.ds(start, half)], energies.at[i], small_sem.at[5 + i]
            )
        )
    int_copies = []
    for tile in range(k_tiles):
        here = pl.ds(tile * TILE, TILE)
        int_copies.append(
            pltpu.make_async_copy(int_hbm.at[here], mine.at[tile], int_sem.at[tile])
        )
    for copy in (*irr_copies, *int_copies, *other_copies):
        copy.start()
    for copy in irr_copies:
        copy.wait()

    def irrep(number):
        return occ_irr[number // tiles_virtual] ^ vir_irr[number % tiles_virtual]

    def count_up(counts, number):
        return counts + lax.shift_left(jnp.int32(1), 8 * irrep(number))

    def count_of(counts, value):
        return lax.shift_right_logical(counts, 8 * value) & 255

    q_irr = [irrep(number) for number in range(nz)]
    worst = jnp.int32(0)
    for part in range(nz):
        counts = jnp.int32(0)
        for tile in range(k_tiles):
            counts = count_up(counts, part * k_tiles + tile)
        for value in q_irr:
            worst = jnp.maximum(worst, count_of(counts, value))
    which = jnp.int32(0)
    for slots in SLOTS:
        which = which + jnp.where(worst > slots, 1, 0)
    wanted = jnp.int32(0)
    for number in range(nz):
        wanted = count_up(wanted, number)
    both = jnp.int32(0)
    for row in range(0, rows, 2):
        first = irrep(row)
        clash = jnp.logical_and(irrep(row + 1) == first, count_of(wanted, first) > 0)
        both = jnp.where(clash, 1, both)
    picked[0] = which + both * (len(SLOTS) + 1)
    choice_copy = pltpu.make_async_copy(picked, choice, small_sem.at[9])
    choice_copy.start()

    for s in range(k_tiles):
        found[s] = 0
    mine_irr = irrep(r // 2)
    place = jnp.int32(0)
    for tile in range(k_tiles):
        found[place] = tile
        place = place + jnp.where(irrep(z * k_tiles + tile) == mine_irr, 1, 0)
    chosen = [found[s] for s in range(k_tiles)]

    for copy in int_copies:
        copy.wait()
    mid = COLS // 2
    for number, slots in enumerate((*SLOTS, k_tiles)):

        @pl.when(which == number)
        def _():
            parts = []
            for s in range(slots):
                tile = mine[chosen[s]]
                parts += [tile[:HALF], tile[HALF:]]
            for i in range(slots):
                one, two = parts[i], parts[i + slots]
                here = pl.ds(i * HALF, HALF)
                packed[0, here] = jnp.concatenate([one[:, :mid], two[:, :mid]], axis=1)
                packed[1, here] = jnp.concatenate([one[:, mid:], two[:, mid:]], axis=1)

    for copy in other_copies:
        copy.wait()
    row_occ = occ_e[r // tiles_virtual]
    col_occ = occ_e[z // tiles_virtual]
    energies[0:2] = energies[0:2] - row_occ
    energies[2:4] = energies[2:4] - col_occ
    choice_copy.wait()


def block_sparse(nz, rows, amplitudes, integrals, occ_irrep, vir_irrep, occ_energy, vir_energy):
    k_tiles = amplitudes.shape[1] // TILE
    vmem = pl.BlockSpec(memory_space=pltpu.VMEM)
    hbm = pl.BlockSpec(memory_space=pltpu.HBM)
    dma = pltpu.SemaphoreType.DMA
    choice, *rest = pl.pallas_call(
        functools.partial(choice_kernel, nz, k_tiles, rows),
        out_shape=[
            jax.ShapeDtypeStruct((1,), jnp.int32),
            jax.ShapeDtypeStruct((2, k_tiles * HALF, COLS), integrals.dtype),
            jax.ShapeDtypeStruct(occ_irrep.shape, jnp.int32),
            jax.ShapeDtypeStruct(vir_irrep.shape, jnp.int32),
            jax.ShapeDtypeStruct((4, TILE // 2), jnp.float32),
        ],
        in_specs=[hbm] * 5,
        out_specs=[hbm, vmem, vmem, vmem, vmem],
        scratch_shapes=[
            pltpu.VMEM((k_tiles, TILE, COLS), jnp.bfloat16),
            pltpu.SMEM(occ_irrep.shape, jnp.int32),
            pltpu.SMEM(vir_irrep.shape, jnp.int32),
            pltpu.SMEM(occ_energy.shape, jnp.float32),
            pltpu.SMEM((k_tiles,), jnp.int32),
            pltpu.SMEM((1,), jnp.int32),
            dma((k_tiles,)),
            dma((10,)),
        ],
    )(integrals, occ_irrep, vir_irrep, occ_energy, vir_energy)
    kinds = [(slots, pairs) for pairs in (1, 2) for slots in (*SLOTS, k_tiles)]
    branches = [
        functools.partial(fused, nz, slots, pairs, number)
        for number, (slots, pairs) in enumerate(kinds)
    ]
    return lax.switch(choice[0], branches, amplitudes, *rest)


def solution(mesh):
    row, col = mesh.shape["row"], mesh.shape["col"]

    def shards(amplitudes, integrals, occ_irrep, vir_irrep, occ_energy, vir_energy):
        args = (amplitudes, integrals, occ_irrep, vir_irrep, occ_energy, vir_energy)
        plain = (
            (row, col) == (8, 4)
            and amplitudes.shape[0] == TILE
            and integrals.shape[1] == COLS
            and vir_energy.shape[0] == TILE * vir_irrep.shape[0]
        )
        return block_sparse(col, row, *args) if plain else general(*args)

    return jax.shard_map(
        shards,
        mesh=mesh,
        in_specs=(P("row", "col"), P("col", "row"), P(), P(), P(), P()),
        out_specs=P("row", "col"),
        check_vma=False,
    )
```

```python
import functools

import jax
import jax.numpy as jnp
from jax import lax
from jax.experimental import pallas as pl
from jax.experimental.pallas import tpu as pltpu
from jax.sharding import PartitionSpec as P

TILE = 256
MESH = pl.DeviceIdType.MESH


def lookup(table, index):
    hits = index[:, None] == jnp.arange(table.shape[0], dtype=jnp.int32)[None, :]
    return jnp.sum(jnp.where(hits, table[None, :], jnp.zeros_like(table)[None, :]), axis=1)


def irreps(first_tile, count, occ_irrep, vir_irrep, tiles_virtual):
    tiles = first_tile + jnp.arange(count, dtype=jnp.int32)
    return jnp.bitwise_xor(
        lookup(occ_irrep, tiles // tiles_virtual), lookup(vir_irrep, tiles % tiles_virtual)
    )


def general(amplitudes, integrals, occ_irrep, vir_irrep, occ_energy, vir_energy):
    tile_size = TILE
    tiles_virtual = vir_irrep.shape[0]
    virtual_count = vir_energy.shape[0]
    p_rows, k_cols = amplitudes.shape
    p_tiles = p_rows // tile_size
    k_tiles = k_cols // tile_size
    row_index = lax.axis_index("row")
    col_index = lax.axis_index("col")
    p_irr = irreps(row_index * p_tiles, p_tiles, occ_irrep, vir_irrep, tiles_virtual)
    k_irr = irreps(col_index * k_tiles, k_tiles, occ_irrep, vir_irrep, tiles_virtual)
    match = p_irr[:, None] == k_irr[None, :]
    masked_amp = (
        amplitudes.reshape(p_tiles, tile_size, k_tiles, tile_size)
        * match[:, None, :, None].astype(jnp.bfloat16)
    ).reshape(p_rows, k_cols)
    piece = lax.all_gather(integrals, "row", axis=1, tiled=True)
    width = piece.shape[1]
    columns = jnp.arange(width, dtype=jnp.int32)
    column_tiles = columns // tile_size
    q_irr = jnp.bitwise_xor(
        lookup(occ_irrep, column_tiles // tiles_virtual),
        lookup(vir_irrep, column_tiles % tiles_virtual),
    )
    keeper = (k_irr[:, None] == q_irr[None, :]).astype(jnp.bfloat16)
    masked_int = (piece.reshape(k_tiles, tile_size, width) * keeper[:, None, :]).reshape(
        k_cols, width
    )
    partial_cycle = jnp.dot(masked_amp, masked_int, preferred_element_type=jnp.float32)
    cycle = lax.psum_scatter(partial_cycle, "col", scatter_dimension=1, tiled=True)
    q_cols = cycle.shape[1]
    row_pairs = row_index * p_rows + jnp.arange(p_rows, dtype=jnp.int32)
    col_pairs = col_index * q_cols + jnp.arange(q_cols, dtype=jnp.int32)
    row_energy = lookup(vir_energy, row_pairs % virtual_count) - lookup(
        occ_energy, row_pairs // virtual_count
    )
    col_energy = lookup(vir_energy, col_pairs % virtual_count) - lookup(
        occ_energy, col_pairs // virtual_count
    )
    return cycle / (row_energy[:, None] + col_energy[None, :])


CHUNKS = 4
COLS = 128
SLOTS = (3, 4, 5)
TOP = 32767.0
HALF = TILE // 2
CODE_ROWS = HALF + 16


def select_tiles(k_irr, irrep, slots):
    tiles = len(k_irr)
    found = [jnp.int32(tiles)] * slots
    count = jnp.int32(0)
    for tile in range(tiles):
        hit = k_irr[tile] == irrep
        found = [
            jnp.where(jnp.logical_and(hit, count == s), tile, found[s]) for s in range(slots)
        ]
        count = count + jnp.where(hit, 1, 0)
    return found


def cycle_kernel(
    nz,
    slots,
    pairs,
    amp_hbm,
    packed,
    occ_irr_in,
    vir_irr_in,
    energies,
    out_ref,
    occ_irr,
    vir_irr,
    table,
    blocks,
    amp,
    own,
    codes,
    in_codes,
    powers,
    other,
    inverse,
    small_sem,
    amp_sem,
    near_send,
    near_recv,
    fwd_send,
    z_send,
    z_recv,
    last_sem,
):
    r = lax.axis_index("row")
    z = lax.axis_index("col")
    core = r % 2
    chip = r // 2
    x = chip % 2
    y = chip // 2
    chip_x = chip + 1 - 2 * x
    chip_y = chip + 2 - 4 * y
    chips = (chip, chip_x, chip_y, chip_x + chip_y - chip)
    xr = 2 * chip_x + core
    yr = 2 * chip_y + core
    sr = r + 1 - 2 * core
    tiles_virtual = vir_irr.shape[0]
    k_tiles = amp_hbm.shape[1] // TILE
    zero_tile = 2 * k_tiles
    depth = slots * HALF
    step = depth // 2

    def remote(src, dst, send_sem, recv_sem, target):
        return pltpu.make_async_remote_copy(
            src_ref=src,
            dst_ref=dst,
            send_sem=send_sem,
            recv_sem=recv_sem,
            device_id=target,
            device_id_type=MESH,
        )

    barrier = pltpu.get_barrier_semaphore()
    for target in (xr, yr, sr):
        pl.semaphore_signal(barrier, inc=1, device_id=(target, z), device_id_type=MESH)
    rows_met = (r,) if pairs == 1 else (r, sr)
    for k in range(1, nz):
        for row in rows_met:
            pl.semaphore_signal(
                barrier, inc=1, device_id=(row, (z + k) % nz), device_id_type=MESH
            )

    irr_copies = [
        pltpu.make_async_copy(occ_irr_in, occ_irr, small_sem.at[0]),
        pltpu.make_async_copy(vir_irr_in, vir_irr, small_sem.at[1]),
    ]
    amp_copies = []
    amp_shares = []
    for tile in range(k_tiles):
        here = pl.ds(tile * TILE, TILE)
        place = amp.at[core * k_tiles + tile]
        amp_copies.append(
            pltpu.make_async_copy(amp_hbm.at[:, here], place, amp_sem.at[0, tile])
        )
        amp_shares.append(
            remote(
                amp_hbm.at[:, here], place, amp_sem.at[1, tile], amp_sem.at[2, tile], (sr, z)
            )
        )
    own_copy = pltpu.make_async_copy(
        packed.at[:, pl.ds(0, depth)], blocks.at[chip], small_sem.at[2]
    )
    for copy in irr_copies:
        copy.start()

    pl.semaphore_wait(barrier, 3 + len(rows_met) * (nz - 1))

    x_order = (0, 1, 2, 3)
    y_order = (1, 0, 3, 2)

    def piece(source, chunk):
        return blocks.at[source, chunk // 2, pl.ds(chunk % 2 * step, step)]

    def near(axis, chunk):
        return remote(
            packed.at[chunk // 2, pl.ds(chunk % 2 * step, step)],
            piece(chip, chunk),
            near_send.at[axis, chunk],
            near_recv.at[axis, chunk],
            ((xr, yr)[axis], z),
        )

    def arrival(rel, chunk):
        ref = piece(chips[rel], chunk)
        return remote(ref, ref, near_send.at[0, chunk], near_recv.at[rel - 1, chunk], (xr, z))

    def forward(chunk):
        source, target = (chip_x, yr) if chunk % 2 == 0 else (chip_y, xr)
        ref = piece(source, chunk)
        return remote(ref, ref, fwd_send.at[chunk], near_recv.at[2, chunk], (target, z))

    for cx, cy in zip(x_order[:3], y_order[:3]):
        near(0, cx).start()
        near(1, cy).start()

    for copy in (*amp_shares, *amp_copies, own_copy):
        copy.start()
    amp[zero_tile] = jnp.zeros((TILE, TILE), jnp.bfloat16)

    for copy in irr_copies:
        copy.wait()

    def irrep(number):
        return occ_irr[number // tiles_virtual] ^ vir_irr[number % tiles_virtual]

    k_irr = [irrep(z * k_tiles + tile) for tile in range(k_tiles)]
    q_irr = [irrep(source) for source in chips]
    first_irr = irrep(2 * chip)
    for rel in range(4):
        chosen = select_tiles(k_irr, q_irr[rel], slots)
        for side in range(pairs):
            row = side if pairs == 2 else jnp.where(first_irr == q_irr[rel], 0, 1)
            for i, tile in enumerate(chosen):
                table[(rel * pairs + side) * slots + i] = jnp.where(
                    tile == k_tiles, zero_tile, row * k_tiles + tile
                )
    own_copy.wait()

    low = lax.broadcasted_iota(jnp.int32, (HALF, COLS), 1) < COLS // 2

    def swap(values):
        return pltpu.roll(values, COLS // 2, 1)

    def chip_of(rel):
        return (x + rel % 2) % 2 + 2 * ((y + rel // 2) % 2)

    def send(rel, side, part, static_part):
        place = 0 if pairs == 1 else core
        row = r if pairs == 1 else 2 * chip + side
        lines = pl.ds(0, HALF if pairs == 2 and static_part == 0 else CODE_ROWS)
        return remote(
            codes.at[rel, side, part, lines],
            in_codes.at[z, place, part, lines],
            z_send.at[rel, side, part],
            z_recv.at[z, place, part],
            (row, chip_of(rel)),
        )

    def share(part):
        given = 0 if pairs == 1 else 1 - core
        return remote(
            own.at[given, part], other.at[part], last_sem.at[0, part], last_sem.at[1, part], (sr, z)
        )

    def multiply(rel, side, part):
        source = chip_of(rel)
        left = jnp.concatenate(
            [amp[table[(rel * pairs + side) * slots + i]] for i in range(slots)], axis=1
        )
        right = blocks[source, part]
        one = jnp.dot(left[:, :depth], right, preferred_element_type=jnp.float32)
        two = jnp.dot(left[:, depth:], right, preferred_element_type=jnp.float32)
        product = jnp.where(
            low, one[:HALF] + swap(two[:HALF]), swap(one[HALF:]) + two[HALF:]
        )

        @pl.when(z == source)
        def _():
            own[side, part] = product

        @pl.when(z != source)
        def _():
            group = 16 if pairs == 1 else 8
            groups = product.reshape(HALF // group, group, COLS)
            most = jnp.maximum(jnp.max(jnp.abs(groups), axis=0), 1e-30)
            power = jnp.ceil(jnp.log2(most))
            scaled = jnp.floor(groups * (TOP * jnp.exp2(-power))[None] + 0.5)
            ints = jnp.clip(scaled, -TOP, TOP).astype(jnp.int32)
            codes[rel, side, part, pl.ds(0, HALF)] = ints.reshape(HALF, COLS).astype(jnp.int16)
            if pairs == 1:
                codes[rel, side, part, pl.ds(HALF, 16)] = power.astype(jnp.int32).astype(
                    jnp.int16
                )
                send(rel, side, part, None).start()
            else:

                @pl.when(part == 0)
                def _():
                    powers[rel, side] = power
                    send(rel, side, part, 0).start()

                @pl.when(part == 1)
                def _():
                    both = jnp.concatenate([powers[rel, side], power], axis=0)
                    codes[rel, side, part, pl.ds(HALF, 16)] = both.astype(jnp.int32).astype(
                        jnp.int16
                    )
                    send(rel, side, part, 1).start()

    def pass_on(*chunks):
        for chunk in chunks:
            arrival(1 + chunk % 2, chunk).wait_recv()
            forward(chunk).start()

    def when(turn, number):
        return pl.when(turn == number)

    def turn_body(step_number, _):
        swapped = jnp.where(step_number == 1, 2, 1)
        turn = jnp.where((step_number + 1) // 2 == 1, swapped, step_number)
        place = (turn + 1) % 3
        rel = jnp.where(turn < 2, 0, jnp.where(place == 2, 3, 2 - place))
        part = jnp.where(turn < 2, turn, (turn + 1) // 3 - 1)

        @when(turn, 2)
        def _():
            arrival(2, 0).wait_recv()

        @when(turn, 3)
        def _():
            arrival(1, 1).wait_recv()

        @when(turn, 4)
        def _():
            pass_on(2, 3)
            arrival(3, 0).wait_recv()
            arrival(3, 1).wait_recv()

        @when(turn, 5)
        def _():
            row_energy = jnp.concatenate([energies[0:1], energies[1:2]], axis=1)
            col_energy = jnp.concatenate([energies[2:3], energies[3:4]], axis=1)
            keep = jnp.where(irrep(r) == irrep(z), 1.0, 0.0).astype(jnp.float32)
            inverse[...] = keep / (jnp.broadcast_to(row_energy, (TILE, TILE)).T + col_energy)
            arrival(2, 2).wait_recv()

        @when(turn, 6)
        def _():
            arrival(1, 3).wait_recv()

        @when(turn, 7)
        def _():
            arrival(3, 2).wait_recv()
            arrival(3, 3).wait_recv()

        for side in range(pairs):
            multiply(rel, side, part)
        if pairs == 2:

            @pl.when(z == chip_of(rel))
            def _():
                share(part).start()

        return 0

    pass_on(0, 1)
    near(0, x_order[3]).start()
    near(1, y_order[3]).start()
    for copy in amp_copies:
        copy.wait()
    for copy in amp_shares:
        copy.wait_recv()
    lax.fori_loop(0, 8, turn_body, 0)

    def arrived(source, place, part):
        lines = pl.ds(0, HALF if pairs == 2 and part == 0 else CODE_ROWS)
        ref = in_codes.at[source, place, part, lines]
        remote(
            ref, ref, z_send.at[0, 0, part], z_recv.at[source, place, part], (r, source)
        ).wait_recv()

    def collect(total, place, part):
        group = 16 if pairs == 1 else 8
        for k in range(1, nz):
            source = (z + k) % nz
            if pairs == 1 or part == 0:
                arrived(source, place, part)
            if pairs == 2 and part == 0:
                arrived(source, place, 1)
            values = in_codes[source, place, part, pl.ds(0, HALF)].astype(jnp.int32)
            values = values.astype(jnp.float32).reshape(HALF // group, group, COLS)
            scale = in_codes[source, place, part if pairs == 1 else 1, pl.ds(HALF, 16)]
            scale = jnp.exp2(scale.astype(jnp.int32).astype(jnp.float32)) * (1.0 / TOP)
            if pairs == 2:
                scale = scale[part * 8 : part * 8 + 8]
            total = total + (values * scale[None]).reshape(HALF, COLS)
        return total

    def put(half_core, first, last):
        here = pl.ds(pl.multiple_of(half_core * COLS, COLS), COLS)
        top = jnp.where(low, first, swap(last))
        bottom = jnp.where(low, swap(first), last)
        out_ref[:HALF, here] = top * inverse[:HALF, here]
        out_ref[HALF:, here] = bottom * inverse[HALF:, here]

    if pairs == 1:
        for part in (0, 1):
            own[0, part] = collect(own[0, part], 0, part)
            share(part).start()
        put(core, own[0, 0], own[0, 1])
        for part in (0, 1):
            share(part).wait_recv()
        put(1 - core, other[0], other[1])
    else:
        for part in (0, 1):
            share(part).wait_recv()
            own[core, part] = collect(own[core, part], core, part)
            other[part] = collect(other[part], 1 - core, part)
        put(core, own[core, 0], own[core, 1])
        put(1 - core, other[0], other[1])

    for rel in range(4):

        @pl.when(z != chips[rel])
        def _():
            for side in range(pairs):
                for part in (0, 1):
                    send(rel, side, part, part).wait_send()

    for chunk in range(CHUNKS):
        near(0, chunk).wait_send()
        near(1, chunk).wait_send()
        forward(chunk).wait_send()
    for part in (0, 1):
        share(part).wait_send()
    for copy in amp_shares:
        copy.wait_send()


def fused(nz, slots, pairs, number, amplitudes, packed, occ_irrep, vir_irrep, energies):
    rows, depth = amplitudes.shape
    k_tiles = depth // TILE
    vmem = pl.BlockSpec(memory_space=pltpu.VMEM)
    hbm = pl.BlockSpec(memory_space=pltpu.HBM)
    dma = pltpu.SemaphoreType.DMA
    return pl.pallas_call(
        functools.partial(cycle_kernel, nz, slots, pairs),
        out_shape=jax.ShapeDtypeStruct((rows, TILE), jnp.float32),
        in_specs=[hbm, vmem, vmem, vmem, vmem],
        out_specs=vmem,
        scratch_shapes=[
            pltpu.SMEM(occ_irrep.shape, jnp.int32),
            pltpu.SMEM(vir_irrep.shape, jnp.int32),
            pltpu.SMEM((4 * pairs * slots,), jnp.int32),
            pltpu.VMEM((4, 2, slots * HALF, COLS), jnp.bfloat16),
            pltpu.VMEM((2 * k_tiles + 1, rows, TILE), jnp.bfloat16),
            pltpu.VMEM((pairs, 2, HALF, COLS), jnp.float32),
            pltpu.VMEM((4, pairs, 2, CODE_ROWS, COLS), jnp.int16),
            pltpu.VMEM((nz, pairs, 2, CODE_ROWS, COLS), jnp.int16),
            pltpu.VMEM((4, 2, 8, COLS), jnp.float32),
            pltpu.VMEM((2, HALF, COLS), jnp.float32),
            pltpu.VMEM((rows, TILE), jnp.float32),
            dma((3,)),
            dma((3, k_tiles)),
            dma((2, CHUNKS)),
            dma((3, CHUNKS)),
            dma((CHUNKS,)),
            dma((4, pairs, 2)),
            dma((nz, pairs, 2)),
            dma((2, 2)),
        ],
        compiler_params=pltpu.CompilerParams(
            collective_id=number, has_side_effects=True, vmem_limit_bytes=40 << 20
        ),
    )(amplitudes, packed, occ_irrep, vir_irrep, energies)


def choice_kernel(
    nz,
    k_tiles,
    rows,
    int_hbm,
    occ_irr_hbm,
    vir_irr_hbm,
    occ_e_hbm,
    vir_e_hbm,
    choice,
    packed,
    occ_irr_out,
    vir_irr_out,
    energies,
    mine,
    occ_irr,
    vir_irr,
    occ_e,
    found,
    picked,
    int_sem,
    small_sem,
):
    r = lax.axis_index("row")
    z = lax.axis_index("col")
    tiles_virtual = vir_irr.shape[0]
    half = TILE // 2
    irr_copies = [
        pltpu.make_async_copy(occ_irr_hbm, occ_irr, small_sem.at[0]),
        pltpu.make_async_copy(vir_irr_hbm, vir_irr, small_sem.at[1]),
    ]
    other_copies = [
        pltpu.make_async_copy(occ_irr_hbm, occ_irr_out, small_sem.at[2]),
        pltpu.make_async_copy(vir_irr_hbm, vir_irr_out, small_sem.at[3]),
        pltpu.make_async_copy(occ_e_hbm, occ_e, small_sem.at[4]),
    ]
    for i in range(4):
        tile = (r if i < 2 else z) % tiles_virtual
        start = pl.multiple_of(tile * TILE + (i % 2) * half, half)
        other_copies.append(
            pltpu.make_async_copy(
                vir_e_hbm.at[pl.ds(start, half)], energies.at[i], small_sem.at[5 + i]
            )
        )
    int_copies = []
    parts = int_sem.shape[0]
    for part in range(parts):
        here = pl.ds(part * (k_tiles // parts) * TILE, k_tiles // parts * TILE)
        int_copies.append(
            pltpu.make_async_copy(int_hbm.at[here], mine.at[here], int_sem.at[part])
        )
    for copy in (*irr_copies, *int_copies, *other_copies):
        copy.start()
    for copy in irr_copies:
        copy.wait()

    def irrep(number):
        return occ_irr[number // tiles_virtual] ^ vir_irr[number % tiles_virtual]

    def count_up(counts, number):
        return counts + lax.shift_left(jnp.int32(1), 8 * irrep(number))

    def count_of(counts, value):
        return lax.shift_right_logical(counts, 8 * value) & 255

    q_irr = [irrep(number) for number in range(nz)]
    worst = jnp.int32(0)
    for part in range(nz):
        counts = jnp.int32(0)
        for tile in range(k_tiles):
            counts = count_up(counts, part * k_tiles + tile)
        for value in q_irr:
            worst = jnp.maximum(worst, count_of(counts, value))
    which = jnp.int32(0)
    for slots in SLOTS:
        which = which + jnp.where(worst > slots, 1, 0)
    wanted = jnp.int32(0)
    for number in range(nz):
        wanted = count_up(wanted, number)
    both = jnp.int32(0)
    for row in range(0, rows, 2):
        first = irrep(row)
        clash = jnp.logical_and(irrep(row + 1) == first, count_of(wanted, first) > 0)
        both = jnp.where(clash, 1, both)
    picked[0] = which + both * (len(SLOTS) + 1)
    choice_copy = pltpu.make_async_copy(picked, choice, small_sem.at[9])
    choice_copy.start()

    for s in range(k_tiles):
        found[s] = 0
    mine_irr = irrep(r // 2)
    place = jnp.int32(0)
    for tile in range(k_tiles):
        found[place] = tile
        place = place + jnp.where(irrep(z * k_tiles + tile) == mine_irr, 1, 0)
    chosen = [found[s] for s in range(k_tiles)]

    for copy in int_copies:
        copy.wait()
    mid = COLS // 2
    for number, slots in enumerate((*SLOTS, k_tiles)):

        @pl.when(which == number)
        def _():
            parts = []
            for s in range(slots):
                tile = mine[pl.ds(pl.multiple_of(chosen[s] * TILE, TILE), TILE)]
                parts += [tile[:HALF], tile[HALF:]]
            for i in range(slots):
                one, two = parts[i], parts[i + slots]
                here = pl.ds(i * HALF, HALF)
                packed[0, here] = jnp.concatenate([one[:, :mid], two[:, :mid]], axis=1)
                packed[1, here] = jnp.concatenate([one[:, mid:], two[:, mid:]], axis=1)

    for copy in other_copies:
        copy.wait()
    row_occ = occ_e[r // tiles_virtual]
    col_occ = occ_e[z // tiles_virtual]
    energies[0:2] = energies[0:2] - row_occ
    energies[2:4] = energies[2:4] - col_occ
    choice_copy.wait()


def block_sparse(nz, rows, amplitudes, integrals, occ_irrep, vir_irrep, occ_energy, vir_energy):
    k_tiles = amplitudes.shape[1] // TILE
    vmem = pl.BlockSpec(memory_space=pltpu.VMEM)
    hbm = pl.BlockSpec(memory_space=pltpu.HBM)
    dma = pltpu.SemaphoreType.DMA
    choice, *rest = pl.pallas_call(
        functools.partial(choice_kernel, nz, k_tiles, rows),
        out_shape=[
            jax.ShapeDtypeStruct((1,), jnp.int32),
            jax.ShapeDtypeStruct((2, k_tiles * HALF, COLS), integrals.dtype),
            jax.ShapeDtypeStruct(occ_irrep.shape, jnp.int32),
            jax.ShapeDtypeStruct(vir_irrep.shape, jnp.int32),
            jax.ShapeDtypeStruct((4, TILE // 2), jnp.float32),
        ],
        in_specs=[hbm] * 5,
        out_specs=[hbm, vmem, vmem, vmem, vmem],
        scratch_shapes=[
            pltpu.VMEM(integrals.shape, jnp.bfloat16),
            pltpu.SMEM(occ_irrep.shape, jnp.int32),
            pltpu.SMEM(vir_irrep.shape, jnp.int32),
            pltpu.SMEM(occ_energy.shape, jnp.float32),
            pltpu.SMEM((k_tiles,), jnp.int32),
            pltpu.SMEM((1,), jnp.int32),
            dma((2,)),
            dma((10,)),
        ],
    )(integrals, occ_irrep, vir_irrep, occ_energy, vir_energy)
    kinds = [(slots, pairs) for pairs in (1, 2) for slots in (*SLOTS, k_tiles)]
    branches = [
        functools.partial(fused, nz, slots, pairs, number)
        for number, (slots, pairs) in enumerate(kinds)
    ]
    return lax.switch(choice[0], branches, amplitudes, *rest)


def solution(mesh):
    row, col = mesh.shape["row"], mesh.shape["col"]

    def shards(amplitudes, integrals, occ_irrep, vir_irrep, occ_energy, vir_energy):
        args = (amplitudes, integrals, occ_irrep, vir_irrep, occ_energy, vir_energy)
        plain = (
            (row, col) == (8, 4)
            and amplitudes.shape[0] == TILE
            and integrals.shape[1] == COLS
            and vir_energy.shape[0] == TILE * vir_irrep.shape[0]
        )
        return block_sparse(col, row, *args) if plain else general(*args)

    return jax.shard_map(
        shards,
        mesh=mesh,
        in_specs=(P("row", "col"), P("col", "row"), P(), P(), P(), P()),
        out_specs=P("row", "col"),
        check_vma=False,
    )
```

```python
import functools

import jax
import jax.numpy as jnp
from jax import lax
from jax.experimental import pallas as pl
from jax.experimental.pallas import tpu as pltpu
from jax.sharding import PartitionSpec as P

TILE = 256
MESH = pl.DeviceIdType.MESH


def lookup(table, index):
    hits = index[:, None] == jnp.arange(table.shape[0], dtype=jnp.int32)[None, :]
    return jnp.sum(jnp.where(hits, table[None, :], jnp.zeros_like(table)[None, :]), axis=1)


def irreps(first_tile, count, occ_irrep, vir_irrep, tiles_virtual):
    tiles = first_tile + jnp.arange(count, dtype=jnp.int32)
    return jnp.bitwise_xor(
        lookup(occ_irrep, tiles // tiles_virtual), lookup(vir_irrep, tiles % tiles_virtual)
    )


def general(amplitudes, integrals, occ_irrep, vir_irrep, occ_energy, vir_energy):
    tile_size = TILE
    tiles_virtual = vir_irrep.shape[0]
    virtual_count = vir_energy.shape[0]
    p_rows, k_cols = amplitudes.shape
    p_tiles = p_rows // tile_size
    k_tiles = k_cols // tile_size
    row_index = lax.axis_index("row")
    col_index = lax.axis_index("col")
    p_irr = irreps(row_index * p_tiles, p_tiles, occ_irrep, vir_irrep, tiles_virtual)
    k_irr = irreps(col_index * k_tiles, k_tiles, occ_irrep, vir_irrep, tiles_virtual)
    match = p_irr[:, None] == k_irr[None, :]
    masked_amp = (
        amplitudes.reshape(p_tiles, tile_size, k_tiles, tile_size)
        * match[:, None, :, None].astype(jnp.bfloat16)
    ).reshape(p_rows, k_cols)
    piece = lax.all_gather(integrals, "row", axis=1, tiled=True)
    width = piece.shape[1]
    columns = jnp.arange(width, dtype=jnp.int32)
    column_tiles = columns // tile_size
    q_irr = jnp.bitwise_xor(
        lookup(occ_irrep, column_tiles // tiles_virtual),
        lookup(vir_irrep, column_tiles % tiles_virtual),
    )
    keeper = (k_irr[:, None] == q_irr[None, :]).astype(jnp.bfloat16)
    masked_int = (piece.reshape(k_tiles, tile_size, width) * keeper[:, None, :]).reshape(
        k_cols, width
    )
    partial_cycle = jnp.dot(masked_amp, masked_int, preferred_element_type=jnp.float32)
    cycle = lax.psum_scatter(partial_cycle, "col", scatter_dimension=1, tiled=True)
    q_cols = cycle.shape[1]
    row_pairs = row_index * p_rows + jnp.arange(p_rows, dtype=jnp.int32)
    col_pairs = col_index * q_cols + jnp.arange(q_cols, dtype=jnp.int32)
    row_energy = lookup(vir_energy, row_pairs % virtual_count) - lookup(
        occ_energy, row_pairs // virtual_count
    )
    col_energy = lookup(vir_energy, col_pairs % virtual_count) - lookup(
        occ_energy, col_pairs // virtual_count
    )
    return cycle / (row_energy[:, None] + col_energy[None, :])


CHUNKS = 4
COLS = 128
SLOTS = (3, 4, 5)
TOP = 32767.0
HALF = TILE // 2
CODE_ROWS = HALF + 16


def select_tiles(k_irr, irrep, slots):
    tiles = len(k_irr)
    found = [jnp.int32(tiles)] * slots
    count = jnp.int32(0)
    for tile in range(tiles):
        hit = k_irr[tile] == irrep
        found = [
            jnp.where(jnp.logical_and(hit, count == s), tile, found[s]) for s in range(slots)
        ]
        count = count + jnp.where(hit, 1, 0)
    return found


def cycle_kernel(
    nz,
    slots,
    pairs,
    amp_hbm,
    packed,
    occ_irr_in,
    vir_irr_in,
    energies,
    out_ref,
    occ_irr,
    vir_irr,
    table,
    blocks,
    amp,
    own,
    codes,
    in_codes,
    powers,
    other,
    inverse,
    small_sem,
    amp_sem,
    near_send,
    near_recv,
    fwd_send,
    z_send,
    z_recv,
    last_sem,
):
    r = lax.axis_index("row")
    z = lax.axis_index("col")
    core = r % 2
    chip = r // 2
    x = chip % 2
    y = chip // 2
    chip_x = chip + 1 - 2 * x
    chip_y = chip + 2 - 4 * y
    chips = (chip, chip_x, chip_y, chip_x + chip_y - chip)
    xr = 2 * chip_x + core
    yr = 2 * chip_y + core
    sr = r + 1 - 2 * core
    tiles_virtual = vir_irr.shape[0]
    k_tiles = amp_hbm.shape[1] // TILE
    zero_tile = 2 * k_tiles
    depth = slots * HALF
    step = depth // 2

    def remote(src, dst, send_sem, recv_sem, target):
        return pltpu.make_async_remote_copy(
            src_ref=src,
            dst_ref=dst,
            send_sem=send_sem,
            recv_sem=recv_sem,
            device_id=target,
            device_id_type=MESH,
        )

    barrier = pltpu.get_barrier_semaphore()
    for target in (xr, yr, sr):
        pl.semaphore_signal(barrier, inc=1, device_id=(target, z), device_id_type=MESH)
    rows_met = (r,) if pairs == 1 else (r, sr)
    for k in range(1, nz):
        for row in rows_met:
            pl.semaphore_signal(
                barrier, inc=1, device_id=(row, (z + k) % nz), device_id_type=MESH
            )

    irr_copies = [
        pltpu.make_async_copy(occ_irr_in, occ_irr, small_sem.at[0]),
        pltpu.make_async_copy(vir_irr_in, vir_irr, small_sem.at[1]),
    ]
    amp_copies = []
    amp_shares = []
    for tile in range(k_tiles):
        here = pl.ds(tile * TILE, TILE)
        place = amp.at[core * k_tiles + tile]
        amp_copies.append(
            pltpu.make_async_copy(amp_hbm.at[:, here], place, amp_sem.at[0, tile])
        )
        amp_shares.append(
            remote(
                amp_hbm.at[:, here], place, amp_sem.at[1, tile], amp_sem.at[2, tile], (sr, z)
            )
        )
    own_copy = pltpu.make_async_copy(
        packed.at[:, pl.ds(0, depth)], blocks.at[chip], small_sem.at[2]
    )
    for copy in irr_copies:
        copy.start()

    pl.semaphore_wait(barrier, 3 + len(rows_met) * (nz - 1))

    x_order = (0, 1, 2, 3)
    y_order = (1, 0, 3, 2)

    def piece(source, chunk):
        return blocks.at[source, chunk // 2, pl.ds(chunk % 2 * step, step)]

    def near(axis, chunk):
        return remote(
            packed.at[chunk // 2, pl.ds(chunk % 2 * step, step)],
            piece(chip, chunk),
            near_send.at[axis, chunk],
            near_recv.at[axis, chunk],
            ((xr, yr)[axis], z),
        )

    def arrival(rel, chunk):
        ref = piece(chips[rel], chunk)
        return remote(ref, ref, near_send.at[0, chunk], near_recv.at[rel - 1, chunk], (xr, z))

    def forward(chunk):
        source, target = (chip_x, yr) if chunk % 2 == 0 else (chip_y, xr)
        ref = piece(source, chunk)
        return remote(ref, ref, fwd_send.at[chunk], near_recv.at[2, chunk], (target, z))

    for cx, cy in zip(x_order[:3], y_order[:3]):
        near(0, cx).start()
        near(1, cy).start()

    for copy in (*amp_shares, *amp_copies, own_copy):
        copy.start()
    amp[zero_tile] = jnp.zeros((TILE, TILE), jnp.bfloat16)

    for copy in irr_copies:
        copy.wait()

    def irrep(number):
        return occ_irr[number // tiles_virtual] ^ vir_irr[number % tiles_virtual]

    k_irr = [irrep(z * k_tiles + tile) for tile in range(k_tiles)]
    q_irr = [irrep(source) for source in chips]
    first_irr = irrep(2 * chip)
    for rel in range(4):
        chosen = select_tiles(k_irr, q_irr[rel], slots)
        for side in range(pairs):
            row = side if pairs == 2 else jnp.where(first_irr == q_irr[rel], 0, 1)
            for i, tile in enumerate(chosen):
                table[(rel * pairs + side) * slots + i] = jnp.where(
                    tile == k_tiles, zero_tile, row * k_tiles + tile
                )
    own_copy.wait()

    low = lax.broadcasted_iota(jnp.int32, (HALF, COLS), 1) < COLS // 2

    def swap(values):
        return pltpu.roll(values, COLS // 2, 1)

    def chip_of(rel):
        return (x + rel % 2) % 2 + 2 * ((y + rel // 2) % 2)

    def send(rel, side, part, static_part):
        place = 0 if pairs == 1 else core
        row = r if pairs == 1 else 2 * chip + side
        lines = pl.ds(0, HALF if pairs == 2 and static_part == 0 else CODE_ROWS)
        return remote(
            codes.at[rel, side, part, lines],
            in_codes.at[z, place, part, lines],
            z_send.at[rel, side, part],
            z_recv.at[z, place, part],
            (row, chip_of(rel)),
        )

    def share(part):
        given = 0 if pairs == 1 else 1 - core
        return remote(
            own.at[given, part], other.at[part], last_sem.at[0, part], last_sem.at[1, part], (sr, z)
        )

    def multiply(rel, side, part):
        source = chip_of(rel)
        left = jnp.concatenate(
            [amp[table[(rel * pairs + side) * slots + i]] for i in range(slots)], axis=1
        )
        right = blocks[source, part]
        one = jnp.dot(left[:, :depth], right, preferred_element_type=jnp.float32)
        two = jnp.dot(left[:, depth:], right, preferred_element_type=jnp.float32)
        product = jnp.where(
            low, one[:HALF] + swap(two[:HALF]), swap(one[HALF:]) + two[HALF:]
        )

        @pl.when(z == source)
        def _():
            own[side, part] = product

        @pl.when(z != source)
        def _():
            group = 16 if pairs == 1 else 8
            groups = product.reshape(HALF // group, group, COLS)
            most = jnp.maximum(jnp.max(jnp.abs(groups), axis=0), 1e-30)
            power = jnp.ceil(jnp.log2(most))
            scaled = jnp.floor(groups * (TOP * jnp.exp2(-power))[None] + 0.5)
            ints = jnp.clip(scaled, -TOP, TOP).astype(jnp.int32)
            codes[rel, side, part, pl.ds(0, HALF)] = ints.reshape(HALF, COLS).astype(jnp.int16)
            if pairs == 1:
                codes[rel, side, part, pl.ds(HALF, 16)] = power.astype(jnp.int32).astype(
                    jnp.int16
                )
                send(rel, side, part, None).start()
            else:

                @pl.when(part == 0)
                def _():
                    powers[rel, side] = power
                    send(rel, side, part, 0).start()

                @pl.when(part == 1)
                def _():
                    both = jnp.concatenate([powers[rel, side], power], axis=0)
                    codes[rel, side, part, pl.ds(HALF, 16)] = both.astype(jnp.int32).astype(
                        jnp.int16
                    )
                    send(rel, side, part, 1).start()

    def pass_on(*chunks):
        for chunk in chunks:
            arrival(1 + chunk % 2, chunk).wait_recv()
            forward(chunk).start()

    def when(turn, number):
        return pl.when(turn == number)

    def turn_body(step_number, _):
        swapped = jnp.where(step_number == 1, 2, 1)
        turn = jnp.where((step_number + 1) // 2 == 1, swapped, step_number)
        place = (turn + 1) % 3
        rel = jnp.where(turn < 2, 0, jnp.where(place == 2, 3, 2 - place))
        part = jnp.where(turn < 2, turn, (turn + 1) // 3 - 1)

        @when(turn, 2)
        def _():
            arrival(2, 0).wait_recv()

        @when(turn, 3)
        def _():
            arrival(1, 1).wait_recv()

        @when(turn, 4)
        def _():
            pass_on(2, 3)
            arrival(3, 0).wait_recv()
            arrival(3, 1).wait_recv()

        @when(turn, 5)
        def _():
            arrival(2, 2).wait_recv()

        @when(turn, 6)
        def _():
            arrival(1, 3).wait_recv()

        @when(turn, 7)
        def _():
            arrival(3, 2).wait_recv()
            arrival(3, 3).wait_recv()

        for side in range(pairs):
            multiply(rel, side, part)
        if pairs == 2:

            @pl.when(z == chip_of(rel))
            def _():
                share(part).start()

        return 0

    row_energy = jnp.concatenate([energies[0:1], energies[1:2]], axis=1)
    col_energy = jnp.concatenate([energies[2:3], energies[3:4]], axis=1)
    keep = jnp.where(irrep(r) == irrep(z), 1.0, 0.0).astype(jnp.float32)
    inverse[...] = keep / (jnp.broadcast_to(row_energy, (TILE, TILE)).T + col_energy)
    pass_on(0, 1)
    near(0, x_order[3]).start()
    near(1, y_order[3]).start()
    for copy in amp_copies:
        copy.wait()
    for copy in amp_shares:
        copy.wait_recv()
    lax.fori_loop(0, 8, turn_body, 0)

    def arrived(source, place, part):
        lines = pl.ds(0, HALF if pairs == 2 and part == 0 else CODE_ROWS)
        ref = in_codes.at[source, place, part, lines]
        remote(
            ref, ref, z_send.at[0, 0, part], z_recv.at[source, place, part], (r, source)
        ).wait_recv()

    def collect(total, place, part):
        group = 16 if pairs == 1 else 8
        for k in range(1, nz):
            source = (z + k) % nz
            if pairs == 1 or part == 0:
                arrived(source, place, part)
            if pairs == 2 and part == 0:
                arrived(source, place, 1)
            values = in_codes[source, place, part, pl.ds(0, HALF)].astype(jnp.int32)
            values = values.astype(jnp.float32).reshape(HALF // group, group, COLS)
            scale = in_codes[source, place, part if pairs == 1 else 1, pl.ds(HALF, 16)]
            scale = jnp.exp2(scale.astype(jnp.int32).astype(jnp.float32)) * (1.0 / TOP)
            if pairs == 2:
                scale = scale[part * 8 : part * 8 + 8]
            total = total + (values * scale[None]).reshape(HALF, COLS)
        return total

    def put(half_core, first, last):
        here = pl.ds(pl.multiple_of(half_core * COLS, COLS), COLS)
        top = jnp.where(low, first, swap(last))
        bottom = jnp.where(low, swap(first), last)
        out_ref[:HALF, here] = top * inverse[:HALF, here]
        out_ref[HALF:, here] = bottom * inverse[HALF:, here]

    if pairs == 1:
        for part in (0, 1):
            own[0, part] = collect(own[0, part], 0, part)
            share(part).start()
        put(core, own[0, 0], own[0, 1])
        for part in (0, 1):
            share(part).wait_recv()
        put(1 - core, other[0], other[1])
    else:
        for part in (0, 1):
            share(part).wait_recv()
            own[core, part] = collect(own[core, part], core, part)
            other[part] = collect(other[part], 1 - core, part)
        put(core, own[core, 0], own[core, 1])
        put(1 - core, other[0], other[1])

    for rel in range(4):

        @pl.when(z != chips[rel])
        def _():
            for side in range(pairs):
                for part in (0, 1):
                    send(rel, side, part, part).wait_send()

    for chunk in range(CHUNKS):
        near(0, chunk).wait_send()
        near(1, chunk).wait_send()
        forward(chunk).wait_send()
    for part in (0, 1):
        share(part).wait_send()
    for copy in amp_shares:
        copy.wait_send()


def fused(nz, slots, pairs, number, amplitudes, packed, occ_irrep, vir_irrep, energies):
    rows, depth = amplitudes.shape
    k_tiles = depth // TILE
    vmem = pl.BlockSpec(memory_space=pltpu.VMEM)
    hbm = pl.BlockSpec(memory_space=pltpu.HBM)
    dma = pltpu.SemaphoreType.DMA
    return pl.pallas_call(
        functools.partial(cycle_kernel, nz, slots, pairs),
        out_shape=jax.ShapeDtypeStruct((rows, TILE), jnp.float32),
        in_specs=[hbm, vmem, vmem, vmem, vmem],
        out_specs=vmem,
        scratch_shapes=[
            pltpu.SMEM(occ_irrep.shape, jnp.int32),
            pltpu.SMEM(vir_irrep.shape, jnp.int32),
            pltpu.SMEM((4 * pairs * slots,), jnp.int32),
            pltpu.VMEM((4, 2, slots * HALF, COLS), jnp.bfloat16),
            pltpu.VMEM((2 * k_tiles + 1, rows, TILE), jnp.bfloat16),
            pltpu.VMEM((pairs, 2, HALF, COLS), jnp.float32),
            pltpu.VMEM((4, pairs, 2, CODE_ROWS, COLS), jnp.int16),
            pltpu.VMEM((nz, pairs, 2, CODE_ROWS, COLS), jnp.int16),
            pltpu.VMEM((4, 2, 8, COLS), jnp.float32),
            pltpu.VMEM((2, HALF, COLS), jnp.float32),
            pltpu.VMEM((rows, TILE), jnp.float32),
            dma((3,)),
            dma((3, k_tiles)),
            dma((2, CHUNKS)),
            dma((3, CHUNKS)),
            dma((CHUNKS,)),
            dma((4, pairs, 2)),
            dma((nz, pairs, 2)),
            dma((2, 2)),
        ],
        compiler_params=pltpu.CompilerParams(
            collective_id=number, has_side_effects=True, vmem_limit_bytes=40 << 20
        ),
    )(amplitudes, packed, occ_irrep, vir_irrep, energies)


def choice_kernel(
    nz,
    k_tiles,
    rows,
    int_hbm,
    occ_irr_hbm,
    vir_irr_hbm,
    occ_e_hbm,
    vir_e_hbm,
    choice,
    packed,
    occ_irr_out,
    vir_irr_out,
    energies,
    mine,
    occ_irr,
    vir_irr,
    occ_e,
    found,
    picked,
    int_sem,
    small_sem,
):
    r = lax.axis_index("row")
    z = lax.axis_index("col")
    tiles_virtual = vir_irr.shape[0]
    half = TILE // 2
    irr_copies = [
        pltpu.make_async_copy(occ_irr_hbm, occ_irr, small_sem.at[0]),
        pltpu.make_async_copy(vir_irr_hbm, vir_irr, small_sem.at[1]),
    ]
    other_copies = [
        pltpu.make_async_copy(occ_irr_hbm, occ_irr_out, small_sem.at[2]),
        pltpu.make_async_copy(vir_irr_hbm, vir_irr_out, small_sem.at[3]),
        pltpu.make_async_copy(occ_e_hbm, occ_e, small_sem.at[4]),
    ]
    for i in range(4):
        tile = (r if i < 2 else z) % tiles_virtual
        start = pl.multiple_of(tile * TILE + (i % 2) * half, half)
        other_copies.append(
            pltpu.make_async_copy(
                vir_e_hbm.at[pl.ds(start, half)], energies.at[i], small_sem.at[5 + i]
            )
        )
    int_copies = []
    parts = int_sem.shape[0]
    for part in range(parts):
        here = pl.ds(part * (k_tiles // parts) * TILE, k_tiles // parts * TILE)
        int_copies.append(
            pltpu.make_async_copy(int_hbm.at[here], mine.at[here], int_sem.at[part])
        )
    for copy in (*irr_copies, *int_copies, *other_copies):
        copy.start()
    for copy in irr_copies:
        copy.wait()

    def irrep(number):
        return occ_irr[number // tiles_virtual] ^ vir_irr[number % tiles_virtual]

    def count_up(counts, number):
        return counts + lax.shift_left(jnp.int32(1), 8 * irrep(number))

    def count_of(counts, value):
        return lax.shift_right_logical(counts, 8 * value) & 255

    q_irr = [irrep(number) for number in range(nz)]
    worst = jnp.int32(0)
    for part in range(nz):
        counts = jnp.int32(0)
        for tile in range(k_tiles):
            counts = count_up(counts, part * k_tiles + tile)
        for value in q_irr:
            worst = jnp.maximum(worst, count_of(counts, value))
    which = jnp.int32(0)
    for slots in SLOTS:
        which = which + jnp.where(worst > slots, 1, 0)
    wanted = jnp.int32(0)
    for number in range(nz):
        wanted = count_up(wanted, number)
    both = jnp.int32(0)
    for row in range(0, rows, 2):
        first = irrep(row)
        clash = jnp.logical_and(irrep(row + 1) == first, count_of(wanted, first) > 0)
        both = jnp.where(clash, 1, both)
    picked[0] = which + both * (len(SLOTS) + 1)
    choice_copy = pltpu.make_async_copy(picked, choice, small_sem.at[9])
    choice_copy.start()

    for s in range(k_tiles):
        found[s] = 0
    mine_irr = irrep(r // 2)
    place = jnp.int32(0)
    for tile in range(k_tiles):
        found[place] = tile
        place = place + jnp.where(irrep(z * k_tiles + tile) == mine_irr, 1, 0)
    chosen = [found[s] for s in range(k_tiles)]

    for copy in int_copies:
        copy.wait()
    mid = COLS // 2
    for number, slots in enumerate((*SLOTS, k_tiles)):

        @pl.when(which == number)
        def _():
            parts = []
            for s in range(slots):
                tile = mine[pl.ds(pl.multiple_of(chosen[s] * TILE, TILE), TILE)]
                parts += [tile[:HALF], tile[HALF:]]
            for i in range(slots):
                one, two = parts[i], parts[i + slots]
                here = pl.ds(i * HALF, HALF)
                packed[0, here] = jnp.concatenate([one[:, :mid], two[:, :mid]], axis=1)
                packed[1, here] = jnp.concatenate([one[:, mid:], two[:, mid:]], axis=1)

    for copy in other_copies:
        copy.wait()
    row_occ = occ_e[r // tiles_virtual]
    col_occ = occ_e[z // tiles_virtual]
    energies[0:2] = energies[0:2] - row_occ
    energies[2:4] = energies[2:4] - col_occ
    choice_copy.wait()


def block_sparse(nz, rows, amplitudes, integrals, occ_irrep, vir_irrep, occ_energy, vir_energy):
    k_tiles = amplitudes.shape[1] // TILE
    vmem = pl.BlockSpec(memory_space=pltpu.VMEM)
    hbm = pl.BlockSpec(memory_space=pltpu.HBM)
    dma = pltpu.SemaphoreType.DMA
    choice, *rest = pl.pallas_call(
        functools.partial(choice_kernel, nz, k_tiles, rows),
        out_shape=[
            jax.ShapeDtypeStruct((1,), jnp.int32),
            jax.ShapeDtypeStruct((2, k_tiles * HALF, COLS), integrals.dtype),
            jax.ShapeDtypeStruct(occ_irrep.shape, jnp.int32),
            jax.ShapeDtypeStruct(vir_irrep.shape, jnp.int32),
            jax.ShapeDtypeStruct((4, TILE // 2), jnp.float32),
        ],
        in_specs=[hbm] * 5,
        out_specs=[hbm, vmem, vmem, vmem, vmem],
        scratch_shapes=[
            pltpu.VMEM(integrals.shape, jnp.bfloat16),
            pltpu.SMEM(occ_irrep.shape, jnp.int32),
            pltpu.SMEM(vir_irrep.shape, jnp.int32),
            pltpu.SMEM(occ_energy.shape, jnp.float32),
            pltpu.SMEM((k_tiles,), jnp.int32),
            pltpu.SMEM((1,), jnp.int32),
            dma((2,)),
            dma((10,)),
        ],
    )(integrals, occ_irrep, vir_irrep, occ_energy, vir_energy)
    kinds = [(slots, pairs) for pairs in (1, 2) for slots in (*SLOTS, k_tiles)]
    branches = [
        functools.partial(fused, nz, slots, pairs, number)
        for number, (slots, pairs) in enumerate(kinds)
    ]
    return lax.switch(choice[0], branches, amplitudes, *rest)


def solution(mesh):
    row, col = mesh.shape["row"], mesh.shape["col"]

    def shards(amplitudes, integrals, occ_irrep, vir_irrep, occ_energy, vir_energy):
        args = (amplitudes, integrals, occ_irrep, vir_irrep, occ_energy, vir_energy)
        plain = (
            (row, col) == (8, 4)
            and amplitudes.shape[0] == TILE
            and integrals.shape[1] == COLS
            and vir_energy.shape[0] == TILE * vir_irrep.shape[0]
        )
        return block_sparse(col, row, *args) if plain else general(*args)

    return jax.shard_map(
        shards,
        mesh=mesh,
        in_specs=(P("row", "col"), P("col", "row"), P(), P(), P(), P()),
        out_specs=P("row", "col"),
        check_vma=False,
    )
```
